128 devices in a mesh: row: 16 (over z, x), col: 8 (over y, core).
Axes of the slice: x: 4, y: 4, z: 4, core: 2. Of those that a mesh axis runs over, the one named last changes fastest.
Arguments:
- slab: float32 [2048, 131072], P('col', 'row'), may hold values from -6 to 6
- stored: float32 [128, 131072], P(('row', 'col')), may hold values from -6 to 6
- owner: int32 [4], replicated, may hold values from 0 to 127
Outputs:
- result: float32 [2048, 131072], P('col', 'row')
The draws below stay inside these ranges and needn't reach their ends.
All inputs are finite; a program needn't handle non-finite values.
Results may differ from the reference program's by a relative error of at most 0.0001.
Values sent between devices are 32-bit elements; how exact they have to be, the bound alone decides.
A program may use at most 192 MiB of HBM per device.

```python
import jax
import jax.numpy as jnp
from jax import lax

ORDER = 131072
EIGVECS = 2048
BAND = 64
GROUPS = 4
N_ROW = 16
N_COL = 8
DEVICES = 128


def plant(drawn, key, least, high):
    index_at = [jax.random.randint(jax.random.fold_in(key, axis), (), 0, length) for axis, length in enumerate(drawn.shape)]
    widest = drawn.shape.index(max(drawn.shape))
    next_to = index_at[:widest] + [(index_at[widest] + 1) % drawn.shape[widest]] + index_at[widest + 1:]
    return drawn.at[tuple(index_at)].set(least).at[tuple(next_to)].set(high)


def level_of(key, dims, shards, least, high):
    def one(axis_at, blocks):
        draws = jax.random.uniform(jax.random.fold_in(jax.random.fold_in(key, 6), axis_at), (blocks,), jnp.float32, least / len(shards), high / len(shards))
        return jnp.repeat(jnp.exp(draws), dims[axis_at] // blocks).reshape((-1,) + (1,) * (len(dims) - axis_at - 1))

    gain = one(*shards[0])
    for cut in shards[1:]:
        gain = gain * one(*cut)
    return gain


def bell_draw(rng, dims, scale, reach, shards=(), held_as=jnp.bfloat16):
    values = scale * jax.random.normal(rng, dims, jnp.float32)
    if shards:
        values = values * level_of(rng, dims, shards, -0.22, 0.18)
    return jnp.clip(values, -reach, reach).astype(held_as)


def setup_inputs(seed: int = 0) -> dict:
    key_of = jax.random.split(jax.random.key(seed), 4)
    slab = bell_draw(key_of[0], (EIGVECS, ORDER), 1.0, 6.0, ((0, 8), (1, 16)), jnp.float32)
    stored = bell_draw(key_of[1], (DEVICES, ORDER), 1.0, 6.0, ((0, 128),), jnp.float32)
    owner = plant(jax.random.randint(key_of[2], (GROUPS,), 0, DEVICES), jax.random.fold_in(key_of[2], 1), 0, DEVICES - 1).astype(jnp.int32)
    return {"slab": slab, "stored": stored, "owner": owner}


def offset_of(group):
    return 1 + (37 * group + 11) % 63


def reference(slab, stored, owner):
    parts = N_ROW
    tiles = ORDER // (parts * BAND)
    count = ORDER // BAND
    span = (count - 1) * BAND
    vectors = []
    for group in range(GROUPS):
        vectors.append(lax.dynamic_index_in_dim(stored, owner[group], 0, keepdims=False))

    def apply_block(block):
        rows = block.shape[0]
        natural = block.reshape(rows, parts, tiles, BAND).transpose(0, 2, 1, 3).reshape(rows, ORDER)
        for group in range(GROUPS):
            start = offset_of(group)
            vwin = vectors[group][start:start + span].reshape(count - 1, BAND)
            tau = 2.0 / (jnp.sum(vwin * vwin, axis=-1) + 1e-6)
            middle = natural[:, start:start + span].reshape(rows, count - 1, BAND)
            inner = jnp.sum(middle * vwin[None], axis=-1)
            middle = middle - (inner * tau[None])[:, :, None] * vwin[None]
            natural = jnp.concatenate([natural[:, :start], middle.reshape(rows, span), natural[:, start + span:]], axis=1)
        return natural.reshape(rows, tiles, parts, BAND).transpose(0, 2, 1, 3).reshape(rows, ORDER)

    blocks = slab.reshape(N_COL, EIGVECS // N_COL, ORDER)
    return lax.map(apply_block, blocks).reshape(EIGVECS, ORDER)
```

```python
import functools

import jax
import jax.numpy as jnp
from jax import lax
from jax.experimental import pallas as pl
from jax.experimental.pallas import tpu as pltpu
from jax.sharding import PartitionSpec as P

BAND = 64
GROUPS = 4
LANES = 128
CHUNKS = 8
WIDE = CHUNKS * LANES
MESH = pl.DeviceIdType.MESH
F32 = jnp.float32
BF16 = jnp.bfloat16


def offset_of(group):
    return 1 + (37 * group + 11) % 63


def segment(group, side):
    return (0, offset_of(group)) if side == 0 else (offset_of(group), BAND)


PAIRS = []
for _g in range(GROUPS):
    for _s in range(2):
        for _h in range(_g):
            for _t in range(2):
                _lo = max(segment(_g, _s)[0], segment(_h, _t)[0])
                _hi = min(segment(_g, _s)[1], segment(_h, _t)[1])
                if _lo < _hi:
                    PAIRS.append((_g, _s, _h, _t, _lo, _hi))


def split(x):
    high = x.astype(BF16)
    return high, (x - high.astype(F32)).astype(BF16)


def spread(vectors):
    lane = lax.broadcasted_iota(jnp.int32, (CHUNKS, WIDE), 1)
    row = lax.broadcasted_iota(jnp.int32, (CHUNKS, WIDE), 0)
    here = (lane // LANES) == row
    within = lane % LANES
    zero = jnp.zeros((CHUNKS, WIDE), F32)
    highs, lows = [], []
    for g in range(GROUPS):
        v = vectors[g]
        high = v.astype(BF16).astype(F32)
        wide_high = jnp.concatenate([high] * CHUNKS, axis=1)
        wide_low = jnp.concatenate([v - high] * CHUNKS, axis=1)
        for s in range(2):
            lo, hi = segment(g, s)
            masks = [
                here & (within >= BAND * par + lo) & (within < BAND * par + hi) for par in range(2)
            ]
            for wide, into in ((wide_high, highs), (wide_low, lows)):
                both = jnp.concatenate([jnp.where(m, wide, zero) for m in masks], axis=0)
                into.append(both.astype(BF16))
    return jnp.concatenate(highs, axis=0), jnp.concatenate(lows, axis=0)


def contract_lanes(a, b):
    return lax.dot_general(a, b, (((1,), (1,)), ((), ())), preferred_element_type=F32)


def coef_kernel(
    parts, cols, owner_ref, stored_ref, slab_ref, coef_ref, vec_ref,
    row_in, slab_in, high_in, low_in, send1, recv1, send2, recv2, recv3,
    raw, square_out, square_in, gram, tau, send4, recv4,
    row_sem, slab_sem, s1, r1, s2, r2, s3, r3, st, rt, s4, r4,
):
    half = cols * CHUNKS
    me = lax.axis_index("row")
    col = lax.axis_index("col")
    left = lax.rem(me + parts - 1, parts)
    right = lax.rem(me + 1, parts)

    row_copy = pltpu.make_async_copy(stored_ref, row_in, row_sem)
    row_copy.start()

    def slab_copy(b):
        return pltpu.make_async_copy(
            slab_ref.at[:, pl.ds(pl.multiple_of(b * WIDE, WIDE), WIDE)], slab_in.at[b], slab_sem.at[b]
        )

    lax.fori_loop(0, cols, lambda b, _: (slab_copy(b).start(), 0)[1], 0)

    row_copy.wait()
    low_lanes = lax.broadcasted_iota(jnp.int32, (half, LANES), 1) < BAND
    for q in range(parts // 2):
        even = row_in[pl.ds(q, half, stride=parts), :]
        odd = row_in[pl.ds(q + parts // 2, half, stride=parts), :]
        send1[2 * q] = jnp.where(low_lanes, even, pltpu.roll(odd, BAND, 1))
        send1[2 * q + 1] = jnp.where(low_lanes, pltpu.roll(even, BAND, 1), odd)
    recv1[me] = send1[me]

    def copy1(to, source):
        return pltpu.make_async_remote_copy(
            src_ref=send1.at[to], dst_ref=recv1.at[source], send_sem=s1.at[to], recv_sem=r1.at[source],
            device_id={"row": to}, device_id_type=MESH,
        )

    def copy2(to, source):
        return pltpu.make_async_remote_copy(
            src_ref=send2.at[to], dst_ref=recv2.at[source], send_sem=s2.at[to], recv_sem=r2.at[source],
            device_id={"col": to}, device_id_type=MESH,
        )

    def copy3(to, source):
        return pltpu.make_async_remote_copy(
            src_ref=recv3.at[source], dst_ref=recv3.at[source], send_sem=s3.at[to], recv_sem=r3.at[source],
            device_id={"col": to}, device_id_type=MESH,
        )

    def others(size, mine, step):
        def body(r, _):
            step(lax.rem(mine + r, size))
            return 0

        lax.fori_loop(1, size, body, 0)

    others(parts, me, lambda to: copy1(to, me).start())

    rows = slab_in.shape[1]

    def split_block(b, _):
        slab_copy(b).wait()

        def split_rows(i, _):
            at = pl.ds(pl.multiple_of(i * 32, 32), 32)
            high, low = split(slab_in[b, at, :])
            high_in[b, at, :] = high
            low_in[b, at, :] = low
            return 0

        return lax.fori_loop(0, rows // 32, split_rows, 0)

    lax.fori_loop(0, cols, split_block, 0)

    others(parts, me, lambda src: copy1(src, src).wait_recv())
    for g in range(GROUPS):
        picked = recv1[owner_ref[g] // cols]
        for to in range(cols):
            send2[to, g] = picked[to * CHUNKS:(to + 1) * CHUNKS, :]
    recv2[col] = send2[col]
    others(cols, col, lambda to: copy2(to, col).start())
    others(cols, col, lambda src: copy2(src, src).wait_recv())
    for g in range(GROUPS):
        recv3[col, g] = recv2[owner_ref[g] % cols, g]
    others(cols, col, lambda to: copy3(to, col).start())
    others(cols, col, lambda src: copy3(src, src).wait_recv())

    vec_ref[...] = recv3[...]
    vectors = [recv3[:, g].reshape(half, LANES) for g in range(GROUPS)]
    lane = lax.broadcasted_iota(jnp.int32, (half, LANES), 1)

    def tile_sums(product, lo, hi):
        keep = [
            jnp.where((lane >= BAND * par + lo) & (lane < BAND * par + hi), product, 0.0)
            for par in range(2)
        ]
        return [jnp.sum(k, axis=1, keepdims=True) for k in keep]

    packed = [jnp.zeros((half, LANES), F32) for _ in range(2)]
    for g in range(GROUPS):
        product = vectors[g] * vectors[g]
        for s in range(2):
            sums = tile_sums(product, *segment(g, s))
            packed = [jnp.where(lane == 2 * g + s, sums[par], packed[par]) for par in range(2)]
    for par in range(2):
        square_out[par] = packed[par]

    def square_copy(way, to):
        return pltpu.make_async_remote_copy(
            src_ref=square_out, dst_ref=square_in.at[way], send_sem=st.at[way], recv_sem=rt.at[way],
            device_id={"row": to}, device_id_type=MESH,
        )

    square_copies = [square_copy(0, left), square_copy(1, right)]
    for c in square_copies:
        c.start()

    def partial(b, _):
        high, low = spread(recv3[b])
        depth = high.shape[0]
        first = contract_lanes(jnp.concatenate([high, low], axis=0), high_in[b])
        second = contract_lanes(high, low_in[b])
        total = first[:depth] + (first[depth:] + second)
        raw[:, pl.ds(pl.multiple_of(b * CHUNKS, CHUNKS), CHUNKS), :] = total.reshape(
            depth // CHUNKS, CHUNKS, total.shape[1]
        )
        return 0

    lax.fori_loop(0, cols, partial, 0)

    for n, (g, s, h, t, lo, hi) in enumerate(PAIRS):
        sums = tile_sums(vectors[g] * vectors[h], lo, hi)
        for par in range(2):
            gram[n, par] = jnp.broadcast_to(sums[par], (half, LANES))

    last = me == parts - 1
    first = me == 0

    def of_next(x):
        after = jnp.stack([x[1], pltpu.roll(x[0], half - 1, 0)])
        return jnp.where(last, after, x)

    def of_previous(x):
        before = jnp.stack([pltpu.roll(x[1], 1, 0), x[0]])
        return jnp.where(first, before, x)

    for c in square_copies:
        c.wait()
    mine = jnp.stack(packed)
    after, before = of_next(square_in[0]), of_previous(square_in[1])
    at = lax.broadcasted_iota(jnp.int32, (2, half, 1), 1)
    parity = lax.broadcasted_iota(jnp.int32, (2, half, 1), 0)
    no_next = last & (at == half - 1) & (parity == 1)
    no_previous = first & (at == 0) & (parity == 0)
    for g in range(GROUPS):
        head, tail = slice(2 * g, 2 * g + 1), slice(2 * g + 1, 2 * g + 2)
        own = jnp.where(no_next, 0.0, 2.0 / (mine[:, :, tail] + after[:, :, head] + 1e-06))
        prior = jnp.where(no_previous, 0.0, 2.0 / (before[:, :, tail] + mine[:, :, head] + 1e-06))
        tau[2 * g] = jnp.broadcast_to(prior, (2, half, LANES))
        tau[2 * g + 1] = jnp.broadcast_to(own, (2, half, LANES))

    def exchange(g, n, way):
        to = left if way == 0 else right
        return pltpu.make_async_remote_copy(
            src_ref=send4.at[g, n, way], dst_ref=recv4.at[g, n, way],
            send_sem=s4.at[g, n, way], recv_sem=r4.at[g, n, way],
            device_id={"row": to}, device_id_type=MESH,
        )

    blocks = rows // LANES

    def finish(g, n):
        at = pl.ds(n * LANES, LANES)
        exchange(g, n, 0).wait_recv()
        exchange(g, n, 1).wait_recv()
        head, tail = send4[g, n, 0], send4[g, n, 1]
        prior = tau[2 * g] * (of_previous(recv4[g, n, 1]) + head)
        own = tau[2 * g + 1] * (tail + of_next(recv4[g, n, 0]))
        for par in range(2):
            coef_ref[4 * g + par, :, at] = prior[par]
            coef_ref[4 * g + 2 + par, :, at] = own[par]

    for g in range(GROUPS):
        for n in range(blocks):
            at = pl.ds(n * LANES, LANES)
            if g:
                finish(g - 1, n)
            for s in range(2):
                for par in range(2):
                    x = raw[4 * g + 2 * s + par, :, at]
                    for k, (pg, ps, h, t, _, _) in enumerate(PAIRS):
                        if (pg, ps) == (g, s):
                            x = x - gram[k, par] * coef_ref[4 * h + 2 * t + par, :, at]
                    send4[g, n, s, par] = x
            exchange(g, n, 0).start()
            exchange(g, n, 1).start()
    for n in range(blocks):
        finish(GROUPS - 1, n)

    others(parts, me, lambda to: copy1(to, me).wait_send())
    others(cols, col, lambda to: copy2(to, col).wait_send())
    others(cols, col, lambda to: copy3(to, col).wait_send())
    for g in range(GROUPS):
        for n in range(blocks):
            exchange(g, n, 0).wait_send()
            exchange(g, n, 1).wait_send()


def coefficients(parts, cols, owner, stored, slab):
    rows, length = slab.shape
    half = length // LANES
    vmem, dma = pltpu.VMEM, pltpu.SemaphoreType.DMA
    blocks = rows // LANES
    piece = (cols, GROUPS, CHUNKS, LANES)
    return pl.pallas_call(
        functools.partial(coef_kernel, parts, cols),
        name="coefficients",
        out_shape=(
            jax.ShapeDtypeStruct((4 * GROUPS, half, rows), F32),
            jax.ShapeDtypeStruct(piece, F32),
        ),
        in_specs=[
            pl.BlockSpec(memory_space=pltpu.SMEM),
            pl.BlockSpec(memory_space=pl.ANY),
            pl.BlockSpec(memory_space=pl.ANY),
        ],
        out_specs=(pl.BlockSpec(memory_space=vmem), pl.BlockSpec(memory_space=vmem)),
        scratch_shapes=[
            vmem(stored.shape, F32),
            vmem((cols, rows, WIDE), F32),
            vmem((cols, rows, WIDE), BF16),
            vmem((cols, rows, WIDE), BF16),
            vmem((parts, half, LANES), F32),
            vmem((parts, half, LANES), F32),
            vmem(piece, F32),
            vmem(piece, F32),
            vmem(piece, F32),
            vmem((4 * GROUPS, half, rows), F32),
            vmem((2, half, LANES), F32),
            vmem((2, 2, half, LANES), F32),
            vmem((len(PAIRS), 2, half, LANES), F32),
            vmem((2 * GROUPS, 2, half, LANES), F32),
            vmem((GROUPS, blocks, 2, 2, half, LANES), F32),
            vmem((GROUPS, blocks, 2, 2, half, LANES), F32),
            dma, dma((cols,)),
            dma((parts,)), dma((parts,)),
            dma((cols,)), dma((cols,)),
            dma((cols,)), dma((cols,)),
            dma((2,)), dma((2,)),
            dma((GROUPS, blocks, 2)), dma((GROUPS, blocks, 2)),
        ],
        compiler_params=pltpu.CompilerParams(
            has_side_effects=True, vmem_limit_bytes=40 * 1024 * 1024
        ),
    )(owner, stored, slab)


def update_kernel(coef_ref, vec_ref, slab_ref, out_ref):
    coef = coef_ref[...]
    turned = coef.reshape(coef.shape[0] * coef.shape[1], coef.shape[2]).T
    high, low = split(turned)
    thigh, tlow = spread(vec_ref[0])
    change = jnp.dot(
        jnp.concatenate([high, high], axis=1), jnp.concatenate([tlow, thigh], axis=0),
        preferred_element_type=F32,
    ) + jnp.dot(low, thigh, preferred_element_type=F32)
    out_ref[...] = slab_ref[...] - change


def update(cols, coef, vec, slab):
    rows, length = slab.shape
    return pl.pallas_call(
        update_kernel,
        name="update",
        grid=(cols,),
        out_shape=jax.ShapeDtypeStruct(slab.shape, F32),
        in_specs=[
            pl.BlockSpec((4 * GROUPS, CHUNKS, rows), lambda b: (0, b, 0)),
            pl.BlockSpec((1, GROUPS, CHUNKS, LANES), lambda b: (b, 0, 0, 0)),
            pl.BlockSpec((rows, WIDE), lambda b: (0, b)),
        ],
        out_specs=pl.BlockSpec((rows, WIDE), lambda b: (0, b)),
        compiler_params=pltpu.CompilerParams(vmem_limit_bytes=24 * 1024 * 1024),
    )(coef, vec, slab)


def shards(parts, cols, slab, stored, owner):
    coef, vec = coefficients(parts, cols, owner, stored.reshape(-1, LANES), slab)
    return update(cols, coef, vec, slab)


def solution(mesh):
    placed = (P("col", "row"), P(("row", "col"), None), P())
    body = functools.partial(shards, mesh.shape["row"], mesh.shape["col"])
    return jax.shard_map(
        body, mesh=mesh, in_specs=placed, out_specs=P("col", "row"), check_vma=False
    )
```

```python
import functools

import jax
import jax.numpy as jnp
from jax import lax
from jax.experimental import pallas as pl
from jax.experimental.pallas import tpu as pltpu
from jax.sharding import PartitionSpec as P

BAND = 64
GROUPS = 4
LANES = 128
CHUNKS = 8
WIDE = CHUNKS * LANES
MESH = pl.DeviceIdType.MESH
F32 = jnp.float32
BF16 = jnp.bfloat16


def offset_of(group):
    return 1 + (37 * group + 11) % 63


def segment(group, side):
    return (0, offset_of(group)) if side == 0 else (offset_of(group), BAND)


PAIRS = []
for _g in range(GROUPS):
    for _s in range(2):
        for _h in range(_g):
            for _t in range(2):
                _lo = max(segment(_g, _s)[0], segment(_h, _t)[0])
                _hi = min(segment(_g, _s)[1], segment(_h, _t)[1])
                if _lo < _hi:
                    PAIRS.append((_g, _s, _h, _t, _lo, _hi))


def split(x):
    high = x.astype(BF16)
    return high, (x - high.astype(F32)).astype(BF16)


def spread(vectors):
    lane = lax.broadcasted_iota(jnp.int32, (CHUNKS, WIDE), 1)
    row = lax.broadcasted_iota(jnp.int32, (CHUNKS, WIDE), 0)
    here = (lane // LANES) == row
    within = lane % LANES
    zero = jnp.zeros((CHUNKS, WIDE), F32)
    highs, lows = [], []
    for g in range(GROUPS):
        v = vectors[g]
        high = v.astype(BF16).astype(F32)
        wide_high = jnp.concatenate([high] * CHUNKS, axis=1)
        wide_low = jnp.concatenate([v - high] * CHUNKS, axis=1)
        for s in range(2):
            lo, hi = segment(g, s)
            masks = [
                here & (within >= BAND * par + lo) & (within < BAND * par + hi) for par in range(2)
            ]
            for wide, into in ((wide_high, highs), (wide_low, lows)):
                both = jnp.concatenate([jnp.where(m, wide, zero) for m in masks], axis=0)
                into.append(both.astype(BF16))
    return jnp.concatenate(highs, axis=0), jnp.concatenate(lows, axis=0)


def contract_lanes(a, b):
    return lax.dot_general(a, b, (((1,), (1,)), ((), ())), preferred_element_type=F32)


def coef_kernel(
    parts, cols, owner_hbm, row_in, slab_ref, coef_ref, vec_ref, slab_in,
    owner_ref, high_in, low_in, send1, recv1, recv3,
    raw, packed, square_out, square_in, gram, tau, send4, recv4,
    owner_sem, slab_sem, s1, r1, s3, r3, st, rt, s4, r4,
):
    half = cols * CHUNKS
    me = lax.axis_index("row")
    col = lax.axis_index("col")
    left = lax.rem(me + parts - 1, parts)
    right = lax.rem(me + 1, parts)

    def others(size, mine, step):
        def body(r, _):
            step(lax.rem(mine + r, size))
            return 0

        lax.fori_loop(1, size, body, 0)

    barrier = pltpu.get_barrier_semaphore()
    devices = parts * cols
    mine = me * cols + col
    others(devices, mine, lambda to: pl.semaphore_signal(
        barrier, inc=1, device_id={"row": to // cols, "col": lax.rem(to, cols)}, device_id_type=MESH))
    owner_copy = pltpu.make_async_copy(owner_hbm, owner_ref, owner_sem)
    owner_copy.start()

    def slab_copy(b):
        return pltpu.make_async_copy(
            slab_ref.at[:, pl.ds(pl.multiple_of(b * WIDE, WIDE), WIDE)], slab_in.at[b], slab_sem.at[b]
        )

    lax.fori_loop(0, cols, lambda b, _: (slab_copy(b).start(), 0)[1], 0)

    low_lanes = lax.broadcasted_iota(jnp.int32, (half, LANES), 1) < BAND
    for q in range(parts // 2):
        even = row_in[pl.ds(q, half, stride=parts), :]
        odd = row_in[pl.ds(q + parts // 2, half, stride=parts), :]
        first_half = jnp.where(low_lanes, even, pltpu.roll(odd, BAND, 1))
        second_half = jnp.where(low_lanes, pltpu.roll(even, BAND, 1), odd)
        send1[pl.ds(2 * q * cols, cols)] = first_half.reshape(cols, CHUNKS, LANES)
        send1[pl.ds((2 * q + 1) * cols, cols)] = second_half.reshape(cols, CHUNKS, LANES)
    recv1[mine] = send1[mine]

    def copy1(to):
        return pltpu.make_async_remote_copy(
            src_ref=send1.at[to], dst_ref=recv1.at[mine], send_sem=s1, recv_sem=r1,
            device_id={"row": to // cols, "col": lax.rem(to, cols)}, device_id_type=MESH,
        )

    def copy3(to, source):
        return pltpu.make_async_remote_copy(
            src_ref=recv3.at[source], dst_ref=recv3.at[source], send_sem=s3.at[to], recv_sem=r3.at[source],
            device_id={"col": to}, device_id_type=MESH,
        )

    pl.semaphore_wait(barrier, devices - 1)
    others(devices, mine, lambda to: copy1(to).start())

    rows = slab_in.shape[1]

    def split_block(b, _):
        slab_copy(b).wait()

        def split_rows(i, _):
            at = pl.ds(pl.multiple_of(i * 32, 32), 32)
            high, low = split(slab_in[b, at, :])
            high_in[b, at, :] = high
            low_in[b, at, :] = low
            return 0

        return lax.fori_loop(0, rows // 32, split_rows, 0)

    lax.fori_loop(0, cols, split_block, 0)

    owner_copy.wait()
    every = recv1.at[pl.ds(0, devices - 1)]
    pltpu.make_async_copy(every, every, r1).wait()
    for g in range(GROUPS):
        recv3[col, g] = recv1[owner_ref[g]]
    others(cols, col, lambda to: copy3(to, col).start())

    lane8 = lax.broadcasted_iota(jnp.int32, (CHUNKS, LANES), 1)

    def piece_sums(product, lane, lo, hi):
        return [
            jnp.sum(
                jnp.where((lane >= BAND * par + lo) & (lane < BAND * par + hi), product, 0.0),
                axis=1, keepdims=True,
            )
            for par in range(2)
        ]

    def partial(b):
        at = pl.ds(pl.multiple_of(b * CHUNKS, CHUNKS), CHUNKS)
        piece = recv3[b]
        high, low = spread(piece)
        depth = high.shape[0]
        one = contract_lanes(jnp.concatenate([high, low], axis=0), high_in[b])
        two = contract_lanes(high, low_in[b])
        total = one[:depth] + (one[depth:] + two)
        raw[:, at, :] = total.reshape(depth // CHUNKS, CHUNKS, total.shape[1])
        squares = [jnp.zeros((CHUNKS, LANES), F32) for _ in range(2)]
        for g in range(GROUPS):
            for s in range(2):
                sums = piece_sums(piece[g] * piece[g], lane8, *segment(g, s))
                squares = [jnp.where(lane8 == 2 * g + s, sums[par], squares[par]) for par in range(2)]
        for par in range(2):
            packed[par, at, :] = squares[par]

    def partial_of(src):
        copy3(src, src).wait_recv()
        partial(src)

    partial(col)
    others(cols, col, partial_of)

    vec_ref[...] = recv3[...]
    vectors = [recv3[:, g].reshape(half, LANES) for g in range(GROUPS)]
    lane = lax.broadcasted_iota(jnp.int32, (half, LANES), 1)

    square_out[...] = jnp.concatenate([packed[0], packed[1]], axis=0).T[:2 * GROUPS, :]

    def square_copy(way, to):
        return pltpu.make_async_remote_copy(
            src_ref=square_out, dst_ref=square_in.at[way], send_sem=st.at[way], recv_sem=rt.at[way],
            device_id={"row": to}, device_id_type=MESH,
        )

    square_copies = [square_copy(0, left), square_copy(1, right)]
    for c in square_copies:
        c.start()

    blocks = rows // LANES
    steps = [(n, par) for n in range(blocks) for par in range(2)]
    last = me == parts - 1
    first = me == 0

    def exchange(g, n, way, par):
        to = left if way == 0 else right
        return pltpu.make_async_remote_copy(
            src_ref=send4.at[g, n, way, par], dst_ref=recv4.at[g, n, way, par],
            send_sem=s4.at[g, n, way, par], recv_sem=r4.at[g, n, way, par],
            device_id={"row": to}, device_id_type=MESH,
        )

    def prepare(g, n, par):
        at = pl.ds(n * LANES, LANES)
        for s in range(2):
            x = raw[4 * g + 2 * s + par, :, at]
            for k, (pg, ps, h, t, _, _) in enumerate(PAIRS):
                if (pg, ps) == (g, s):
                    x = x - gram[k, par] * coef_ref[4 * h + 2 * t + par, :, at]
            send4[g, n, s, par] = x
        exchange(g, n, 0, par).start()
        exchange(g, n, 1, par).start()

    def of_next(x, par):
        return jnp.where(last, pltpu.roll(x, half - 1, 0), x) if par else x

    def of_previous(x, par):
        return x if par else jnp.where(first, pltpu.roll(x, 1, 0), x)

    def next_parity(par):
        return jnp.where(last, 1 - par, par)

    def previous_parity(par):
        return jnp.where(first, 1 - par, par)

    def finish(g, n, par):
        at = pl.ds(n * LANES, LANES)
        after, before = next_parity(par), previous_parity(par)
        exchange(g, n, 0, after).wait_recv()
        exchange(g, n, 1, before).wait_recv()
        head, tail = send4[g, n, 0, par], send4[g, n, 1, par]
        coef_ref[4 * g + par, :, at] = tau[2 * g, par] * (of_previous(recv4[g, n, 1, before], par) + head)
        coef_ref[4 * g + 2 + par, :, at] = tau[2 * g + 1, par] * (tail + of_next(recv4[g, n, 0, after], par))

    for n, par in steps:
        prepare(0, n, par)

    for k, (g, s, h, t, lo, hi) in enumerate(PAIRS):
        sums = piece_sums(vectors[g] * vectors[h], lane, lo, hi)
        for par in range(2):
            gram[k, par] = jnp.broadcast_to(sums[par], (half, LANES))

    for c in square_copies:
        c.wait()

    def turned(way):
        full = jnp.concatenate([square_in[way]] * (2 * half // (2 * GROUPS)), axis=0).T
        return [full[:half], full[half:]]

    right_squares, left_squares = turned(0), turned(1)
    at = lax.broadcasted_iota(jnp.int32, (half, 1), 0)
    for par in range(2):
        after = of_next(jnp.where(last, right_squares[1 - par], right_squares[par]), par)
        before = of_previous(jnp.where(first, left_squares[1 - par], left_squares[par]), par)
        here = packed[par]
        for g in range(GROUPS):
            head, tail = slice(2 * g, 2 * g + 1), slice(2 * g + 1, 2 * g + 2)
            own = 2.0 / (here[:, tail] + after[:, head] + 1e-06)
            prior = 2.0 / (before[:, tail] + here[:, head] + 1e-06)
            if par:
                own = jnp.where(last & (at == half - 1), 0.0, own)
            else:
                prior = jnp.where(first & (at == 0), 0.0, prior)
            tau[2 * g, par] = jnp.broadcast_to(prior, (half, LANES))
            tau[2 * g + 1, par] = jnp.broadcast_to(own, (half, LANES))

    for g in range(GROUPS):
        for n, par in steps:
            finish(g, n, par)
            if g + 1 < GROUPS:
                prepare(g + 1, n, par)

    sent = send1.at[pl.ds(0, devices - 1)]
    pltpu.make_async_copy(sent, sent, s1).wait()
    others(cols, col, lambda to: copy3(to, col).wait_send())
    for g in range(GROUPS):
        for n, par in steps:
            exchange(g, n, 0, par).wait_send()
            exchange(g, n, 1, par).wait_send()


def coefficients(parts, cols, owner, stored, slab):
    rows, length = slab.shape
    half = length // LANES
    vmem, dma = pltpu.VMEM, pltpu.SemaphoreType.DMA
    blocks = rows // LANES
    piece = (cols, GROUPS, CHUNKS, LANES)
    return pl.pallas_call(
        functools.partial(coef_kernel, parts, cols),
        name="coefficients",
        out_shape=(
            jax.ShapeDtypeStruct((4 * GROUPS, half, rows), F32),
            jax.ShapeDtypeStruct(piece, F32),
            jax.ShapeDtypeStruct((cols, rows, WIDE), F32),
        ),
        in_specs=[
            pl.BlockSpec(memory_space=pltpu.HBM),
            pl.BlockSpec(memory_space=vmem),
            pl.BlockSpec(memory_space=pltpu.HBM),
        ],
        out_specs=(pl.BlockSpec(memory_space=vmem),) * 3,
        scratch_shapes=[
            pltpu.SMEM((GROUPS,), jnp.int32),
            vmem((cols, rows, WIDE), BF16),
            vmem((cols, rows, WIDE), BF16),
            vmem((parts * cols, CHUNKS, LANES), F32),
            vmem((parts * cols, CHUNKS, LANES), F32),
            vmem(piece, F32),
            vmem((4 * GROUPS, half, rows), F32),
            vmem((2, half, LANES), F32),
            vmem((2 * GROUPS, 2 * half), F32),
            vmem((2, 2 * GROUPS, 2 * half), F32),
            vmem((len(PAIRS), 2, half, LANES), F32),
            vmem((2 * GROUPS, 2, half, LANES), F32),
            vmem((GROUPS, blocks, 2, 2, half, LANES), F32),
            vmem((GROUPS, blocks, 2, 2, half, LANES), F32),
            dma, dma((cols,)),
            dma, dma,
            dma((cols,)), dma((cols,)),
            dma((2,)), dma((2,)),
            dma((GROUPS, blocks, 2, 2)), dma((GROUPS, blocks, 2, 2)),
        ],
        compiler_params=pltpu.CompilerParams(
            has_side_effects=True, collective_id=0, vmem_limit_bytes=40 * 1024 * 1024
        ),
    )(owner, stored, slab)


def update_kernel(cols, coef_ref, vec_ref, slab_ref, out_ref, ready, sem):
    slots = ready.shape[0]

    def copy(b):
        slot = lax.rem(b, slots)
        at = pl.ds(pl.multiple_of(b * WIDE, WIDE), WIDE)
        return pltpu.make_async_copy(ready.at[slot], out_ref.at[:, at], sem.at[slot])

    def block(b, _):
        @pl.when(b >= slots)
        def _():
            copy(b - slots).wait()

        coef = coef_ref[:, pl.ds(pl.multiple_of(b * CHUNKS, CHUNKS), CHUNKS), :]
        turned = coef.reshape(coef.shape[0] * coef.shape[1], coef.shape[2]).T
        high, low = split(turned)
        thigh, tlow = spread(vec_ref[b])
        change = jnp.dot(
            jnp.concatenate([high, high], axis=1), jnp.concatenate([tlow, thigh], axis=0),
            preferred_element_type=F32,
        ) + jnp.dot(low, thigh, preferred_element_type=F32)
        ready[lax.rem(b, slots)] = slab_ref[b] - change
        copy(b).start()
        return 0

    lax.fori_loop(0, cols, block, 0)
    lax.fori_loop(max(cols - slots, 0), cols, lambda b, _: (copy(b).wait(), 0)[1], 0)


def update(cols, coef, vec, slab_in):
    blocks, rows, wide = slab_in.shape
    return pl.pallas_call(
        functools.partial(update_kernel, cols),
        name="update",
        out_shape=jax.ShapeDtypeStruct((rows, blocks * wide), F32),
        in_specs=[pl.BlockSpec(memory_space=pltpu.VMEM)] * 3,
        out_specs=pl.BlockSpec(memory_space=pltpu.HBM),
        scratch_shapes=[pltpu.VMEM((3, rows, wide), F32), pltpu.SemaphoreType.DMA((3,))],
        compiler_params=pltpu.CompilerParams(vmem_limit_bytes=24 * 1024 * 1024),
    )(coef, vec, slab_in)


def shards(parts, cols, slab, stored, owner):
    coef, vec, slab_in = coefficients(parts, cols, owner, stored.reshape(-1, LANES), slab)
    return update(cols, coef, vec, slab_in)


def solution(mesh):
    placed = (P("col", "row"), P(("row", "col"), None), P())
    body = functools.partial(shards, mesh.shape["row"], mesh.shape["col"])
    return jax.shard_map(
        body, mesh=mesh, in_specs=placed, out_specs=P("col", "row"), check_vma=False
    )
```

```python
import functools

import jax
import jax.numpy as jnp
from jax import lax
from jax.experimental import pallas as pl
from jax.experimental.pallas import tpu as pltpu
from jax.sharding import PartitionSpec as P

BAND = 64
GROUPS = 4
LANES = 128
CHUNKS = 8
WIDE = CHUNKS * LANES
PIECES = 2
MESH = pl.DeviceIdType.MESH
F32 = jnp.float32
BF16 = jnp.bfloat16


def offset_of(group):
    return 1 + (37 * group + 11) % 63


def segment(group, side):
    return (0, offset_of(group)) if side == 0 else (offset_of(group), BAND)


PAIRS = []
for _g in range(GROUPS):
    for _s in range(2):
        for _h in range(_g):
            for _t in range(2):
                _lo = max(segment(_g, _s)[0], segment(_h, _t)[0])
                _hi = min(segment(_g, _s)[1], segment(_h, _t)[1])
                if _lo < _hi:
                    PAIRS.append((_g, _s, _h, _t, _lo, _hi))


def split(x):
    high = x.astype(BF16)
    return high, (x - high.astype(F32)).astype(BF16)


def spread(vectors):
    lane = lax.broadcasted_iota(jnp.int32, (CHUNKS, WIDE), 1)
    row = lax.broadcasted_iota(jnp.int32, (CHUNKS, WIDE), 0)
    here = (lane // LANES) == row
    within = lane % LANES
    zero = jnp.zeros((CHUNKS, WIDE), F32)
    highs, lows = [], []
    for g in range(GROUPS):
        v = vectors[g]
        high = v.astype(BF16).astype(F32)
        wide_high = jnp.concatenate([high] * CHUNKS, axis=1)
        wide_low = jnp.concatenate([v - high] * CHUNKS, axis=1)
        for s in range(2):
            lo, hi = segment(g, s)
            masks = [
                here & (within >= BAND * par + lo) & (within < BAND * par + hi) for par in range(2)
            ]
            for wide, into in ((wide_high, highs), (wide_low, lows)):
                both = jnp.concatenate([jnp.where(m, wide, zero) for m in masks], axis=0)
                into.append(both.astype(BF16))
    return jnp.concatenate(highs, axis=0), jnp.concatenate(lows, axis=0)


def contract_lanes(a, b):
    return lax.dot_general(a, b, (((1,), (1,)), ((), ())), preferred_element_type=F32)


def coef_kernel(
    parts, cols, owner_hbm, stored_ref, slab_ref, coef_ref, vec_ref, slab_in,
    owner_ref, row_in, high_in, low_in, send1, recv1, recv3,
    raw, packed, square_out, square_in, gram, tau, send4, recv4,
    owner_sem, row_sem, slab_sem, s1, r1, s3, r3, st, rt, s4, r4,
):
    half = cols * CHUNKS
    me = lax.axis_index("row")
    col = lax.axis_index("col")
    left = lax.rem(me + parts - 1, parts)
    right = lax.rem(me + 1, parts)

    def others(size, mine, step):
        def body(r, _):
            step(lax.rem(mine + r, size))
            return 0

        lax.fori_loop(1, size, body, 0)

    barrier = pltpu.get_barrier_semaphore()
    devices = parts * cols
    mine = me * cols + col
    others(devices, mine, lambda to: pl.semaphore_signal(
        barrier, inc=1, device_id={"row": to // cols, "col": lax.rem(to, cols)}, device_id_type=MESH))
    owner_copy = pltpu.make_async_copy(owner_hbm, owner_ref, owner_sem)
    owner_copy.start()
    row_copy = pltpu.make_async_copy(stored_ref, row_in, row_sem)
    row_copy.start()

    def slab_copy(b):
        return pltpu.make_async_copy(
            slab_ref.at[:, pl.ds(pl.multiple_of(b * WIDE, WIDE), WIDE)], slab_in.at[b], slab_sem.at[b]
        )

    lax.fori_loop(0, cols, lambda b, _: (slab_copy(b).start(), 0)[1], 0)

    row_copy.wait()
    low_lanes = lax.broadcasted_iota(jnp.int32, (half, LANES), 1) < BAND
    for q in range(parts // 2):
        even = row_in[pl.ds(q, half, stride=parts), :]
        odd = row_in[pl.ds(q + parts // 2, half, stride=parts), :]
        first_half = jnp.where(low_lanes, even, pltpu.roll(odd, BAND, 1))
        second_half = jnp.where(low_lanes, pltpu.roll(even, BAND, 1), odd)
        send1[pl.ds(2 * q * cols, cols)] = first_half.reshape(cols, CHUNKS, LANES)
        send1[pl.ds((2 * q + 1) * cols, cols)] = second_half.reshape(cols, CHUNKS, LANES)
    recv1[mine] = send1[mine]

    def copy1(to):
        return pltpu.make_async_remote_copy(
            src_ref=send1.at[to], dst_ref=recv1.at[mine], send_sem=s1, recv_sem=r1,
            device_id={"row": to // cols, "col": lax.rem(to, cols)}, device_id_type=MESH,
        )

    def copy3(to, source):
        return pltpu.make_async_remote_copy(
            src_ref=recv3.at[source], dst_ref=recv3.at[source], send_sem=s3.at[to], recv_sem=r3.at[source],
            device_id={"col": to}, device_id_type=MESH,
        )

    pl.semaphore_wait(barrier, devices - 1)
    others(devices, mine, lambda to: copy1(to).start())

    rows = slab_in.shape[1]

    def split_block(b, _):
        slab_copy(b).wait()

        def split_rows(i, _):
            at = pl.ds(pl.multiple_of(i * 32, 32), 32)
            high, low = split(slab_in[b, at, :])
            high_in[b, at, :] = high
            low_in[b, at, :] = low
            return 0

        return lax.fori_loop(0, rows // 32, split_rows, 0)

    lax.fori_loop(0, cols, split_block, 0)

    owner_copy.wait()
    every = recv1.at[pl.ds(0, devices - 1)]
    pltpu.make_async_copy(every, every, r1).wait()
    for g in range(GROUPS):
        recv3[col, g] = recv1[owner_ref[g]]
    others(cols, col, lambda to: copy3(to, col).start())

    lane8 = lax.broadcasted_iota(jnp.int32, (CHUNKS, LANES), 1)

    def piece_sums(product, lane, lo, hi):
        return [
            jnp.sum(
                jnp.where((lane >= BAND * par + lo) & (lane < BAND * par + hi), product, 0.0),
                axis=1, keepdims=True,
            )
            for par in range(2)
        ]

    def partial(b):
        at = pl.ds(pl.multiple_of(b * CHUNKS, CHUNKS), CHUNKS)
        piece = recv3[b]
        high, low = spread(piece)
        depth = high.shape[0]
        one = contract_lanes(jnp.concatenate([high, low], axis=0), high_in[b])
        two = contract_lanes(high, low_in[b])
        total = one[:depth] + (one[depth:] + two)
        raw[:, at, :] = total.reshape(depth // CHUNKS, CHUNKS, total.shape[1])
        squares = [jnp.zeros((CHUNKS, LANES), F32) for _ in range(2)]
        for g in range(GROUPS):
            for s in range(2):
                sums = piece_sums(piece[g] * piece[g], lane8, *segment(g, s))
                squares = [jnp.where(lane8 == 2 * g + s, sums[par], squares[par]) for par in range(2)]
        for par in range(2):
            packed[par, at, :] = squares[par]

    pair = (col // 2) * 2
    copy3(lax.rem(col, 2) * -2 + 1 + col, lax.rem(col, 2) * -2 + 1 + col).wait_recv()
    partial(pair)
    partial(pair + 1)

    def partial_pair(i, _):
        src = lax.rem(pair + 2 * i, cols)
        copy3(src, src).wait_recv()
        copy3(src + 1, src + 1).wait_recv()
        partial(src)
        partial(src + 1)
        return 0

    lax.fori_loop(1, cols // 2, partial_pair, 0)

    vec_ref[...] = recv3[...]
    vectors = [recv3[:, g].reshape(half, LANES) for g in range(GROUPS)]
    lane = lax.broadcasted_iota(jnp.int32, (half, LANES), 1)

    square_out[...] = jnp.concatenate([packed[0], packed[1]], axis=0).T[:2 * GROUPS, :]

    def square_copy(way, to):
        return pltpu.make_async_remote_copy(
            src_ref=square_out, dst_ref=square_in.at[way], send_sem=st.at[way], recv_sem=rt.at[way],
            device_id={"row": to}, device_id_type=MESH,
        )

    square_copies = [square_copy(0, left), square_copy(1, right)]
    for c in square_copies:
        c.start()

    blocks = rows // LANES
    part = half // PIECES
    steps = [(n, q, par) for n in range(blocks) for q in range(PIECES) for par in range(2)]
    last = me == parts - 1
    first = me == 0

    def exchange(g, n, way, par, q):
        to = left if way == 0 else right
        at = pl.ds(q * part, part)
        return pltpu.make_async_remote_copy(
            src_ref=send4.at[g, n, way, par, at], dst_ref=recv4.at[g, n, way, par, at],
            send_sem=s4.at[g, n, way, par, q], recv_sem=r4.at[g, n, way, par, q],
            device_id={"row": to}, device_id_type=MESH,
        )

    def prepare(g, n, q, par):
        at = pl.ds(n * LANES, LANES)
        tiles = pl.ds(q * part, part)
        for s in range(2):
            x = raw[4 * g + 2 * s + par, tiles, at]
            for k, (pg, ps, h, t, _, _) in enumerate(PAIRS):
                if (pg, ps) == (g, s):
                    x = x - gram[k, par, tiles] * coef_ref[4 * h + 2 * t + par, tiles, at]
            send4[g, n, s, par, tiles] = x
        exchange(g, n, 0, par, q).start()
        exchange(g, n, 1, par, q).start()

    def of_next(x, par):
        return jnp.where(last, pltpu.roll(x, half - 1, 0), x) if par else x

    def of_previous(x, par):
        return x if par else jnp.where(first, pltpu.roll(x, 1, 0), x)

    def next_parity(par):
        return jnp.where(last, 1 - par, par)

    def previous_parity(par):
        return jnp.where(first, 1 - par, par)

    def heads_after(g, n, q, par):
        from_ref = recv4.at[g, n, 0, next_parity(par)]
        if par == 0:
            exchange(g, n, 0, next_parity(par), q).wait_recv()
            return from_ref[q * part:(q + 1) * part]

        @pl.when(jnp.logical_not(last))
        def _():
            exchange(g, n, 0, 1, q).wait_recv()

        @pl.when(last)
        def _():
            if q == 0:
                exchange(g, n, 0, 0, 0).wait_recv()
            if q + 1 < PIECES:
                exchange(g, n, 0, 0, q + 1).wait_recv()

        def shifted():
            if q + 1 < PIECES:
                return from_ref[q * part + 1:(q + 1) * part + 1]
            return pltpu.roll(from_ref[q * part:(q + 1) * part], part - 1, 0)

        return lax.cond(last, shifted, lambda: from_ref[q * part:(q + 1) * part])

    def tails_before(g, n, q, par):
        from_ref = recv4.at[g, n, 1, previous_parity(par)]
        exchange(g, n, 1, previous_parity(par), q).wait_recv()
        if par:
            return from_ref[q * part:(q + 1) * part]

        def shifted():
            if q:
                return from_ref[q * part - 1:(q + 1) * part - 1]
            return pltpu.roll(from_ref[0:part], 1, 0)

        return lax.cond(first, shifted, lambda: from_ref[q * part:(q + 1) * part])

    def finish(g, n, q, par):
        at = pl.ds(n * LANES, LANES)
        tiles = pl.ds(q * part, part)
        after = heads_after(g, n, q, par)
        before = tails_before(g, n, q, par)
        head, tail = send4[g, n, 0, par, tiles], send4[g, n, 1, par, tiles]
        coef_ref[4 * g + par, tiles, at] = tau[2 * g, par, tiles] * (before + head)
        coef_ref[4 * g + 2 + par, tiles, at] = tau[2 * g + 1, par, tiles] * (tail + after)

    for n, q, par in steps:
        prepare(0, n, q, par)

    for k, (g, s, h, t, lo, hi) in enumerate(PAIRS):
        sums = piece_sums(vectors[g] * vectors[h], lane, lo, hi)
        for par in range(2):
            gram[k, par] = jnp.broadcast_to(sums[par], (half, LANES))

    for c in square_copies:
        c.wait()

    def turned(way):
        full = jnp.concatenate([square_in[way]] * (2 * half // (2 * GROUPS)), axis=0).T
        return [full[:half], full[half:]]

    right_squares, left_squares = turned(0), turned(1)
    at = lax.broadcasted_iota(jnp.int32, (half, 1), 0)
    for par in range(2):
        after = of_next(jnp.where(last, right_squares[1 - par], right_squares[par]), par)
        before = of_previous(jnp.where(first, left_squares[1 - par], left_squares[par]), par)
        here = packed[par]
        for g in range(GROUPS):
            head, tail = slice(2 * g, 2 * g + 1), slice(2 * g + 1, 2 * g + 2)
            own = 2.0 / (here[:, tail] + after[:, head] + 1e-06)
            prior = 2.0 / (before[:, tail] + here[:, head] + 1e-06)
            if par:
                own = jnp.where(last & (at == half - 1), 0.0, own)
            else:
                prior = jnp.where(first & (at == 0), 0.0, prior)
            tau[2 * g, par] = jnp.broadcast_to(prior, (half, LANES))
            tau[2 * g + 1, par] = jnp.broadcast_to(own, (half, LANES))

    for g in range(GROUPS):
        for n, q, par in steps:
            finish(g, n, q, par)
            if g + 1 < GROUPS:
                prepare(g + 1, n, q, par)

    sent = send1.at[pl.ds(0, devices - 1)]
    pltpu.make_async_copy(sent, sent, s1).wait()
    others(cols, col, lambda to: copy3(to, col).wait_send())
    for g in range(GROUPS):
        for n, q, par in steps:
            exchange(g, n, 0, par, q).wait_send()
            exchange(g, n, 1, par, q).wait_send()


def coefficients(parts, cols, owner, stored, slab):
    rows, length = slab.shape
    half = length // LANES
    vmem, dma = pltpu.VMEM, pltpu.SemaphoreType.DMA
    blocks = rows // LANES
    piece = (cols, GROUPS, CHUNKS, LANES)
    return pl.pallas_call(
        functools.partial(coef_kernel, parts, cols),
        name="coefficients",
        out_shape=(
            jax.ShapeDtypeStruct((4 * GROUPS, half, rows), F32),
            jax.ShapeDtypeStruct(piece, F32),
            jax.ShapeDtypeStruct((cols, rows, WIDE), F32),
        ),
        in_specs=[
            pl.BlockSpec(memory_space=pltpu.HBM),
            pl.BlockSpec(memory_space=pltpu.HBM),
            pl.BlockSpec(memory_space=pltpu.HBM),
        ],
        out_specs=(pl.BlockSpec(memory_space=vmem),) * 3,
        scratch_shapes=[
            pltpu.SMEM((GROUPS,), jnp.int32),
            vmem(stored.shape, F32),
            vmem((cols, rows, WIDE), BF16),
            vmem((cols, rows, WIDE), BF16),
            vmem((parts * cols, CHUNKS, LANES), F32),
            vmem((parts * cols, CHUNKS, LANES), F32),
            vmem(piece, F32),
            vmem((4 * GROUPS, half, rows), F32),
            vmem((2, half, LANES), F32),
            vmem((2 * GROUPS, 2 * half), F32),
            vmem((2, 2 * GROUPS, 2 * half), F32),
            vmem((len(PAIRS), 2, half, LANES), F32),
            vmem((2 * GROUPS, 2, half, LANES), F32),
            vmem((GROUPS, blocks, 2, 2, half, LANES), F32),
            vmem((GROUPS, blocks, 2, 2, half, LANES), F32),
            dma, dma, dma((cols,)),
            dma, dma,
            dma((cols,)), dma((cols,)),
            dma((2,)), dma((2,)),
            dma((GROUPS, blocks, 2, 2, PIECES)), dma((GROUPS, blocks, 2, 2, PIECES)),
        ],
        compiler_params=pltpu.CompilerParams(
            has_side_effects=True, collective_id=0, vmem_limit_bytes=40 * 1024 * 1024
        ),
    )(*(pltpu.with_memory_space_constraint(x, pltpu.HBM) for x in (owner, stored, slab)))


def update_kernel(cols, coef_ref, vec_ref, slab_ref, out_ref, ready, sem):
    slots = ready.shape[0]

    def copy(b):
        slot = lax.rem(b, slots)
        at = pl.ds(pl.multiple_of(b * WIDE, WIDE), WIDE)
        return pltpu.make_async_copy(ready.at[slot], out_ref.at[:, at], sem.at[slot])

    def block(b):
        coef = coef_ref[:, pl.ds(pl.multiple_of(b * CHUNKS, CHUNKS), CHUNKS), :]
        turned = coef.reshape(coef.shape[0] * coef.shape[1], coef.shape[2]).T
        high, low = split(turned)
        thigh, tlow = spread(vec_ref[b])
        change = jnp.dot(
            jnp.concatenate([high, high], axis=1), jnp.concatenate([tlow, thigh], axis=0),
            preferred_element_type=F32,
        ) + jnp.dot(low, thigh, preferred_element_type=F32)
        ready[lax.rem(b, slots)] = slab_ref[b] - change

    def two(i, _):
        @pl.when(i >= slots // 2)
        def _():
            copy(2 * i - slots).wait()
            copy(2 * i + 1 - slots).wait()

        block(2 * i)
        block(2 * i + 1)
        copy(2 * i).start()
        copy(2 * i + 1).start()
        return 0

    lax.fori_loop(0, cols // 2, two, 0)
    lax.fori_loop(max(cols - slots, 0), cols, lambda b, _: (copy(b).wait(), 0)[1], 0)


def update(cols, coef, vec, slab_in):
    blocks, rows, wide = slab_in.shape
    return pl.pallas_call(
        functools.partial(update_kernel, cols),
        name="update",
        out_shape=jax.ShapeDtypeStruct((rows, blocks * wide), F32),
        in_specs=[pl.BlockSpec(memory_space=pltpu.VMEM)] * 3,
        out_specs=pl.BlockSpec(memory_space=pltpu.HBM),
        scratch_shapes=[pltpu.VMEM((4, rows, wide), F32), pltpu.SemaphoreType.DMA((4,))],
        compiler_params=pltpu.CompilerParams(vmem_limit_bytes=24 * 1024 * 1024),
    )(coef, vec, slab_in)


def shards(parts, cols, slab, stored, owner):
    coef, vec, slab_in = coefficients(parts, cols, owner, stored.reshape(-1, LANES), slab)
    return update(cols, coef, vec, slab_in)


def solution(mesh):
    placed = (P("col", "row"), P(("row", "col"), None), P())
    body = functools.partial(shards, mesh.shape["row"], mesh.shape["col"])
    return jax.shard_map(
        body, mesh=mesh, in_specs=placed, out_specs=P("col", "row"), check_vma=False
    )
```

```python
import functools

import jax
import jax.numpy as jnp
from jax import lax
from jax.experimental import pallas as pl
from jax.experimental.pallas import tpu as pltpu
from jax.sharding import PartitionSpec as P

BAND = 64
GROUPS = 4
LANES = 128
CHUNKS = 8
WIDE = CHUNKS * LANES
PIECES = 2
MESH = pl.DeviceIdType.MESH
F32 = jnp.float32
BF16 = jnp.bfloat16


def offset_of(group):
    return 1 + (37 * group + 11) % 63


def segment(group, side):
    return (0, offset_of(group)) if side == 0 else (offset_of(group), BAND)


PAIRS = []
for _g in range(GROUPS):
    for _s in range(2):
        for _h in range(_g):
            for _t in range(2):
                _lo = max(segment(_g, _s)[0], segment(_h, _t)[0])
                _hi = min(segment(_g, _s)[1], segment(_h, _t)[1])
                if _lo < _hi:
                    PAIRS.append((_g, _s, _h, _t, _lo, _hi))


def split(x):
    high = x.astype(BF16)
    return high, (x - high.astype(F32)).astype(BF16)


def spread(vectors):
    lane = lax.broadcasted_iota(jnp.int32, (CHUNKS, WIDE), 1)
    row = lax.broadcasted_iota(jnp.int32, (CHUNKS, WIDE), 0)
    here = (lane // LANES) == row
    within = lane % LANES
    zero = jnp.zeros((CHUNKS, WIDE), F32)
    highs, lows = [], []
    for g in range(GROUPS):
        v = vectors[g]
        high = v.astype(BF16).astype(F32)
        wide_high = jnp.concatenate([high] * CHUNKS, axis=1)
        wide_low = jnp.concatenate([v - high] * CHUNKS, axis=1)
        for s in range(2):
            lo, hi = segment(g, s)
            masks = [
                here & (within >= BAND * par + lo) & (within < BAND * par + hi) for par in range(2)
            ]
            for wide, into in ((wide_high, highs), (wide_low, lows)):
                both = jnp.concatenate([jnp.where(m, wide, zero) for m in masks], axis=0)
                into.append(both.astype(BF16))
    return jnp.concatenate(highs, axis=0), jnp.concatenate(lows, axis=0)


def contract_lanes(a, b):
    return lax.dot_general(a, b, (((1,), (1,)), ((), ())), preferred_element_type=F32)


def coef_kernel(
    parts, cols, owner_hbm, stored_ref, slab_ref, coef_ref, vec_ref, slab_in,
    owner_ref, row_in, high_in, low_in, send_a, recv_a, send_b, recv_b, pick_a, from_a, pick_b, from_b, recv3,
    raw, packed, square_out, square_in, gram, tau, send4, recv4,
    owner_sem, row_sem, slab_sem, sa, ra, sb, rb, spa, rpa, spb, rpb, s3, r3, st, rt, s4, r4,
):
    half = cols * CHUNKS
    me = lax.axis_index("row")
    col = lax.axis_index("col")
    left = lax.rem(me + parts - 1, parts)
    right = lax.rem(me + 1, parts)

    def others(size, mine, step):
        def body(r, _):
            step(lax.rem(mine + r, size))
            return 0

        lax.fori_loop(1, size, body, 0)

    barrier = pltpu.get_barrier_semaphore()
    others(parts, me, lambda to: pl.semaphore_signal(
        barrier, inc=1, device_id={"row": to}, device_id_type=MESH))
    others(cols, col, lambda to: pl.semaphore_signal(
        barrier, inc=1, device_id={"col": to}, device_id_type=MESH))
    owner_copy = pltpu.make_async_copy(owner_hbm, owner_ref, owner_sem)
    owner_copy.start()
    row_copy = pltpu.make_async_copy(stored_ref, row_in, row_sem)
    row_copy.start()

    def slab_copy(b):
        return pltpu.make_async_copy(
            slab_ref.at[:, pl.ds(pl.multiple_of(b * WIDE, WIDE), WIDE)], slab_in.at[b], slab_sem.at[b]
        )

    lax.fori_loop(0, cols, lambda b, _: (slab_copy(b).start(), 0)[1], 0)

    row_copy.wait()
    low_lanes = lax.broadcasted_iota(jnp.int32, (half, LANES), 1) < BAND
    for q in range(parts // 2):
        even = row_in[pl.ds(q, half, stride=parts), :]
        odd = row_in[pl.ds(q + parts // 2, half, stride=parts), :]
        first_half = jnp.where(low_lanes, even, pltpu.roll(odd, BAND, 1))
        second_half = jnp.where(low_lanes, pltpu.roll(even, BAND, 1), odd)
        for p, mixed in ((2 * q, first_half), (2 * q + 1, second_half)):
            pieces = mixed.reshape(cols // 2, 2, CHUNKS, LANES)
            send_a[p] = pieces[:, 0]
            send_b[:, p] = pieces[:, 1]

    odd = lax.rem(col, 2) == 1

    def copy_a(to):
        return pltpu.make_async_remote_copy(
            src_ref=send_a.at[to], dst_ref=recv_a.at[me], send_sem=sa, recv_sem=ra,
            device_id={"row": to}, device_id_type=MESH,
        )

    def copy_b(i):
        return pltpu.make_async_remote_copy(
            src_ref=send_b.at[i], dst_ref=recv_b.at[col], send_sem=sb.at[i], recv_sem=rb,
            device_id={"col": 2 * i + 1}, device_id_type=MESH,
        )

    def pick_copy_a(i):
        return pltpu.make_async_remote_copy(
            src_ref=pick_a.at[i], dst_ref=from_a.at[col], send_sem=spa.at[i], recv_sem=rpa,
            device_id={"col": 2 * i}, device_id_type=MESH,
        )

    def pick_copy_b(to):
        return pltpu.make_async_remote_copy(
            src_ref=pick_b.at[to], dst_ref=from_b.at[me], send_sem=spb, recv_sem=rpb,
            device_id={"row": to}, device_id_type=MESH,
        )

    def each_other(parity, step):
        def body(r, _):
            i = lax.rem(col // 2 + r, cols // 2)

            @pl.when(2 * i + parity != col)
            def _():
                step(i)

            return 0

        lax.fori_loop(0, cols // 2, body, 0)

    def wait_for(ref, count, sem):
        taken = ref.at[pl.ds(0, count)]
        pltpu.make_async_copy(taken, taken, sem).wait()

    def copy3(to, source):
        return pltpu.make_async_remote_copy(
            src_ref=recv3.at[source], dst_ref=recv3.at[source], send_sem=s3.at[to], recv_sem=r3.at[source],
            device_id={"col": to}, device_id_type=MESH,
        )

    pl.semaphore_wait(barrier, parts + cols - 2)
    each_other(1, lambda i: copy_b(i).start())
    others(parts, me, lambda to: copy_a(to).start())
    recv_a[me] = send_a[me]

    @pl.when(odd)
    def _():
        recv_b[col] = send_b[col // 2]


    rows = slab_in.shape[1]

    def split_block(b, _):
        slab_copy(b).wait()

        def split_rows(i, _):
            at = pl.ds(pl.multiple_of(i * 32, 32), 32)
            high, low = split(slab_in[b, at, :])
            high_in[b, at, :] = high
            low_in[b, at, :] = low
            return 0

        return lax.fori_loop(0, rows // 32, split_rows, 0)

    lax.fori_loop(0, cols, split_block, 0)

    owner_copy.wait()
    @pl.when(odd)
    def _():
        wait_for(recv_b, cols - 1, rb)
        for g in range(GROUPS):
            pick_b[:, g] = recv_b[lax.rem(owner_ref[g], cols)]
        from_b[me] = pick_b[me]
        others(parts, me, lambda to: pick_copy_b(to).start())

    wait_for(recv_a, parts - 1, ra)
    for g in range(GROUPS):
        pick_a[:, g] = recv_a[owner_ref[g] // cols]
    each_other(0, lambda i: pick_copy_a(i).start())

    @pl.when(odd)
    def _():
        wait_for(from_b, parts - 1, rpb)
        for g in range(GROUPS):
            recv3[col, g] = from_b[owner_ref[g] // cols, g]

    @pl.when(jnp.logical_not(odd))
    def _():
        from_a[col] = pick_a[col // 2]
        wait_for(from_a, cols - 1, rpa)
        for g in range(GROUPS):
            recv3[col, g] = from_a[lax.rem(owner_ref[g], cols), g]

    others(cols, col, lambda to: copy3(to, col).start())

    lane8 = lax.broadcasted_iota(jnp.int32, (CHUNKS, LANES), 1)

    def piece_sums(product, lane, lo, hi):
        return [
            jnp.sum(
                jnp.where((lane >= BAND * par + lo) & (lane < BAND * par + hi), product, 0.0),
                axis=1, keepdims=True,
            )
            for par in range(2)
        ]

    def partial(b):
        at = pl.ds(pl.multiple_of(b * CHUNKS, CHUNKS), CHUNKS)
        piece = recv3[b]
        high, low = spread(piece)
        depth = high.shape[0]
        one = contract_lanes(jnp.concatenate([high, low], axis=0), high_in[b])
        two = contract_lanes(high, low_in[b])
        total = one[:depth] + (one[depth:] + two)
        raw[:, at, :] = total.reshape(depth // CHUNKS, CHUNKS, total.shape[1])
        squares = [jnp.zeros((CHUNKS, LANES), F32) for _ in range(2)]
        for g in range(GROUPS):
            for s in range(2):
                sums = piece_sums(piece[g] * piece[g], lane8, *segment(g, s))
                squares = [jnp.where(lane8 == 2 * g + s, sums[par], squares[par]) for par in range(2)]
        for par in range(2):
            packed[par, at, :] = squares[par]

    pair = (col // 2) * 2
    copy3(lax.rem(col, 2) * -2 + 1 + col, lax.rem(col, 2) * -2 + 1 + col).wait_recv()
    partial(pair)
    partial(pair + 1)

    def partial_pair(i, _):
        src = lax.rem(pair + 2 * i, cols)
        copy3(src, src).wait_recv()
        copy3(src + 1, src + 1).wait_recv()
        partial(src)
        partial(src + 1)
        return 0

    lax.fori_loop(1, cols // 2, partial_pair, 0)

    vec_ref[...] = recv3[...]
    vectors = [recv3[:, g].reshape(half, LANES) for g in range(GROUPS)]
    lane = lax.broadcasted_iota(jnp.int32, (half, LANES), 1)

    square_out[...] = jnp.concatenate([packed[0], packed[1]], axis=0).T[:2 * GROUPS, :]

    def square_copy(way, to):
        return pltpu.make_async_remote_copy(
            src_ref=square_out, dst_ref=square_in.at[way], send_sem=st.at[way], recv_sem=rt.at[way],
            device_id={"row": to}, device_id_type=MESH,
        )

    square_copies = [square_copy(0, left), square_copy(1, right)]
    for c in square_copies:
        c.start()

    blocks = rows // LANES
    part = half // PIECES
    steps = [(n, q, par) for n in range(blocks) for q in range(PIECES) for par in range(2)]
    last = me == parts - 1
    first = me == 0

    def exchange(g, n, way, par, q):
        to = left if way == 0 else right
        at = pl.ds(q * part, part)
        return pltpu.make_async_remote_copy(
            src_ref=send4.at[g, n, way, par, at], dst_ref=recv4.at[g, n, way, par, at],
            send_sem=s4.at[g, n, way, par, q], recv_sem=r4.at[g, n, way, par, q],
            device_id={"row": to}, device_id_type=MESH,
        )

    def prepare(g, n, q, par):
        at = pl.ds(n * LANES, LANES)
        tiles = pl.ds(q * part, part)
        for s in range(2):
            x = raw[4 * g + 2 * s + par, tiles, at]
            for k, (pg, ps, h, t, _, _) in enumerate(PAIRS):
                if (pg, ps) == (g, s):
                    x = x - gram[k, par, tiles] * coef_ref[4 * h + 2 * t + par, tiles, at]
            send4[g, n, s, par, tiles] = x
        exchange(g, n, 0, par, q).start()
        exchange(g, n, 1, par, q).start()

    def of_next(x, par):
        return jnp.where(last, pltpu.roll(x, half - 1, 0), x) if par else x

    def of_previous(x, par):
        return x if par else jnp.where(first, pltpu.roll(x, 1, 0), x)

    def next_parity(par):
        return jnp.where(last, 1 - par, par)

    def previous_parity(par):
        return jnp.where(first, 1 - par, par)

    def heads_after(g, n, q, par):
        from_ref = recv4.at[g, n, 0, next_parity(par)]
        if par == 0:
            exchange(g, n, 0, next_parity(par), q).wait_recv()
            return from_ref[q * part:(q + 1) * part]

        @pl.when(jnp.logical_not(last))
        def _():
            exchange(g, n, 0, 1, q).wait_recv()

        @pl.when(last)
        def _():
            if q == 0:
                exchange(g, n, 0, 0, 0).wait_recv()
            if q + 1 < PIECES:
                exchange(g, n, 0, 0, q + 1).wait_recv()

        def shifted():
            if q + 1 < PIECES:
                return from_ref[q * part + 1:(q + 1) * part + 1]
            return pltpu.roll(from_ref[q * part:(q + 1) * part], part - 1, 0)

        return lax.cond(last, shifted, lambda: from_ref[q * part:(q + 1) * part])

    def tails_before(g, n, q, par):
        from_ref = recv4.at[g, n, 1, previous_parity(par)]
        exchange(g, n, 1, previous_parity(par), q).wait_recv()
        if par:
            return from_ref[q * part:(q + 1) * part]

        def shifted():
            if q:
                return from_ref[q * part - 1:(q + 1) * part - 1]
            return pltpu.roll(from_ref[0:part], 1, 0)

        return lax.cond(first, shifted, lambda: from_ref[q * part:(q + 1) * part])

    def finish(g, n, q, par):
        at = pl.ds(n * LANES, LANES)
        tiles = pl.ds(q * part, part)
        after = heads_after(g, n, q, par)
        before = tails_before(g, n, q, par)
        head, tail = send4[g, n, 0, par, tiles], send4[g, n, 1, par, tiles]
        coef_ref[4 * g + par, tiles, at] = tau[2 * g, par, tiles] * (before + head)
        coef_ref[4 * g + 2 + par, tiles, at] = tau[2 * g + 1, par, tiles] * (tail + after)

    for n, q, par in steps:
        prepare(0, n, q, par)

    for k, (g, s, h, t, lo, hi) in enumerate(PAIRS):
        sums = piece_sums(vectors[g] * vectors[h], lane, lo, hi)
        for par in range(2):
            gram[k, par] = jnp.broadcast_to(sums[par], (half, LANES))

    for c in square_copies:
        c.wait()

    def turned(way):
        full = jnp.concatenate([square_in[way]] * (2 * half // (2 * GROUPS)), axis=0).T
        return [full[:half], full[half:]]

    right_squares, left_squares = turned(0), turned(1)
    at = lax.broadcasted_iota(jnp.int32, (half, 1), 0)
    for par in range(2):
        after = of_next(jnp.where(last, right_squares[1 - par], right_squares[par]), par)
        before = of_previous(jnp.where(first, left_squares[1 - par], left_squares[par]), par)
        here = packed[par]
        for g in range(GROUPS):
            head, tail = slice(2 * g, 2 * g + 1), slice(2 * g + 1, 2 * g + 2)
            own = 2.0 / (here[:, tail] + after[:, head] + 1e-06)
            prior = 2.0 / (before[:, tail] + here[:, head] + 1e-06)
            if par:
                own = jnp.where(last & (at == half - 1), 0.0, own)
            else:
                prior = jnp.where(first & (at == 0), 0.0, prior)
            tau[2 * g, par] = jnp.broadcast_to(prior, (half, LANES))
            tau[2 * g + 1, par] = jnp.broadcast_to(own, (half, LANES))

    for g in range(GROUPS):
        for n, q, par in steps:
            finish(g, n, q, par)
            if g + 1 < GROUPS:
                prepare(g + 1, n, q, par)

    wait_for(send_a, parts - 1, sa)
    each_other(1, lambda i: copy_b(i).wait_send())
    each_other(0, lambda i: pick_copy_a(i).wait_send())

    @pl.when(odd)
    def _():
        wait_for(pick_b, parts - 1, spb)

    others(cols, col, lambda to: copy3(to, col).wait_send())
    for g in range(GROUPS):
        for n, q, par in steps:
            exchange(g, n, 0, par, q).wait_send()
            exchange(g, n, 1, par, q).wait_send()


def coefficients(parts, cols, owner, stored, slab):
    rows, length = slab.shape
    half = length // LANES
    vmem, dma = pltpu.VMEM, pltpu.SemaphoreType.DMA
    blocks = rows // LANES
    piece = (cols, GROUPS, CHUNKS, LANES)
    return pl.pallas_call(
        functools.partial(coef_kernel, parts, cols),
        name="coefficients",
        out_shape=(
            jax.ShapeDtypeStruct((4 * GROUPS, half, rows), F32),
            jax.ShapeDtypeStruct(piece, F32),
            jax.ShapeDtypeStruct((cols, rows, WIDE), F32),
        ),
        in_specs=[
            pl.BlockSpec(memory_space=pltpu.HBM),
            pl.BlockSpec(memory_space=pltpu.HBM),
            pl.BlockSpec(memory_space=pltpu.HBM),
        ],
        out_specs=(pl.BlockSpec(memory_space=vmem),) * 3,
        scratch_shapes=[
            pltpu.SMEM((GROUPS,), jnp.int32),
            vmem(stored.shape, F32),
            vmem((cols, rows, WIDE), BF16),
            vmem((cols, rows, WIDE), BF16),
            vmem((parts, cols // 2, CHUNKS, LANES), F32),
            vmem((parts, cols // 2, CHUNKS, LANES), F32),
            vmem((cols // 2, parts, CHUNKS, LANES), F32),
            vmem((cols, parts, CHUNKS, LANES), F32),
            vmem((cols // 2, GROUPS, CHUNKS, LANES), F32),
            vmem((cols, GROUPS, CHUNKS, LANES), F32),
            vmem((parts, GROUPS, CHUNKS, LANES), F32),
            vmem((parts, GROUPS, CHUNKS, LANES), F32),
            vmem(piece, F32),
            vmem((4 * GROUPS, half, rows), F32),
            vmem((2, half, LANES), F32),
            vmem((2 * GROUPS, 2 * half), F32),
            vmem((2, 2 * GROUPS, 2 * half), F32),
            vmem((len(PAIRS), 2, half, LANES), F32),
            vmem((2 * GROUPS, 2, half, LANES), F32),
            vmem((GROUPS, blocks, 2, 2, half, LANES), F32),
            vmem((GROUPS, blocks, 2, 2, half, LANES), F32),
            dma, dma, dma((cols,)),
            dma, dma, dma((cols // 2,)), dma,
            dma((cols // 2,)), dma, dma, dma,
            dma((cols,)), dma((cols,)),
            dma((2,)), dma((2,)),
            dma((GROUPS, blocks, 2, 2, PIECES)), dma((GROUPS, blocks, 2, 2, PIECES)),
        ],
        compiler_params=pltpu.CompilerParams(
            has_side_effects=True, collective_id=0, vmem_limit_bytes=40 * 1024 * 1024
        ),
    )(*(pltpu.with_memory_space_constraint(x, pltpu.HBM) for x in (owner, stored, slab)))


def update_kernel(cols, coef_ref, vec_ref, slab_ref, out_ref, ready, sem):
    slots = ready.shape[0]

    def copy(b):
        slot = lax.rem(b, slots)
        at = pl.ds(pl.multiple_of(b * WIDE, WIDE), WIDE)
        return pltpu.make_async_copy(ready.at[slot], out_ref.at[:, at], sem.at[slot])

    def block(b):
        coef = coef_ref[:, pl.ds(pl.multiple_of(b * CHUNKS, CHUNKS), CHUNKS), :]
        turned = coef.reshape(coef.shape[0] * coef.shape[1], coef.shape[2]).T
        high, low = split(turned)
        thigh, tlow = spread(vec_ref[b])
        change = jnp.dot(
            jnp.concatenate([high, high], axis=1), jnp.concatenate([tlow, thigh], axis=0),
            preferred_element_type=F32,
        ) + jnp.dot(low, thigh, preferred_element_type=F32)
        ready[lax.rem(b, slots)] = slab_ref[b] - change

    def two(i, _):
        @pl.when(i >= slots // 2)
        def _():
            copy(2 * i - slots).wait()
            copy(2 * i + 1 - slots).wait()

        block(2 * i)
        block(2 * i + 1)
        copy(2 * i).start()
        copy(2 * i + 1).start()
        return 0

    lax.fori_loop(0, cols // 2, two, 0)
    lax.fori_loop(max(cols - slots, 0), cols, lambda b, _: (copy(b).wait(), 0)[1], 0)


def update(cols, coef, vec, slab_in):
    blocks, rows, wide = slab_in.shape
    return pl.pallas_call(
        functools.partial(update_kernel, cols),
        name="update",
        out_shape=jax.ShapeDtypeStruct((rows, blocks * wide), F32),
        in_specs=[pl.BlockSpec(memory_space=pltpu.VMEM)] * 3,
        out_specs=pl.BlockSpec(memory_space=pltpu.HBM),
        scratch_shapes=[pltpu.VMEM((4, rows, wide), F32), pltpu.SemaphoreType.DMA((4,))],
        compiler_params=pltpu.CompilerParams(vmem_limit_bytes=24 * 1024 * 1024),
    )(coef, vec, slab_in)


def shards(parts, cols, slab, stored, owner):
    coef, vec, slab_in = coefficients(parts, cols, owner, stored.reshape(-1, LANES), slab)
    return update(cols, coef, vec, slab_in)


def solution(mesh):
    placed = (P("col", "row"), P(("row", "col"), None), P())
    body = functools.partial(shards, mesh.shape["row"], mesh.shape["col"])
    return jax.shard_map(
        body, mesh=mesh, in_specs=placed, out_specs=P("col", "row"), check_vma=False
    )
```

```python
import functools

import jax
import jax.numpy as jnp
from jax import lax
from jax.experimental import pallas as pl
from jax.experimental.pallas import tpu as pltpu
from jax.sharding import PartitionSpec as P

BAND = 64
GROUPS = 4
LANES = 128
CHUNKS = 8
WIDE = CHUNKS * LANES
SUMS = 4 * GROUPS
PAIR = 2 * LANES
PIECES = 2
MESH = pl.DeviceIdType.MESH
F32 = jnp.float32
BF16 = jnp.bfloat16


def offset_of(group):
    return 1 + (37 * group + 11) % 63


def segment(group, side):
    return (0, offset_of(group)) if side == 0 else (offset_of(group), BAND)


PAIRS = []
for _g in range(GROUPS):
    for _s in range(2):
        for _h in range(_g):
            for _t in range(2):
                _lo = max(segment(_g, _s)[0], segment(_h, _t)[0])
                _hi = min(segment(_g, _s)[1], segment(_h, _t)[1])
                if _lo < _hi:
                    PAIRS.append((_g, _s, _h, _t, _lo, _hi))


def split(x):
    high = x.astype(BF16)
    return high, (x - high.astype(F32)).astype(BF16)


def spread(vectors):
    shape = (SUMS, LANES)
    lane = lax.broadcasted_iota(jnp.int32, shape, 1)
    line = lax.broadcasted_iota(jnp.int32, shape, 0)
    group = line // 4
    at = lane - BAND * lax.rem(line, 2)
    keep = jnp.zeros(shape, jnp.bool_)
    for g in range(GROUPS):
        for s in range(2):
            lo, hi = segment(g, s)
            keep = keep | ((line // 2 == 2 * g + s) & (at >= lo) & (at < hi))
    none = jnp.zeros(shape, BF16)
    halves = []
    for i in range(CHUNKS):
        rows = [jnp.broadcast_to(vectors[g][i:i + 1, :], shape) for g in range(GROUPS)]
        own = rows[0]
        for g in range(1, GROUPS):
            own = jnp.where(group == g, rows[g], own)
        halves.append(split(jnp.where(keep, own, 0.0)))
    pairs = []
    for i in range(0, CHUNKS, 2):
        first, second = halves[i], halves[i + 1]
        lines = []
        for term in range(2):
            lines.append(jnp.concatenate([first[term], none], axis=1))
            lines.append(jnp.concatenate([none, second[term]], axis=1))
        pairs.append(jnp.concatenate(lines, axis=0))
    return pairs


def contract_lanes(a, b):
    return lax.dot_general(a, b, (((1,), (1,)), ((), ())), preferred_element_type=F32)


def coef_kernel(
    parts, cols, owner_hbm, stored_ref, slab_ref, coef_ref, spread_ref, slab_in,
    owner_ref, row_in, high_in, low_in, send_a, recv_a, send_b, recv_b, pick_a, from_a, pick_b, from_b, recv3,
    raw, packed, square_out, square_in, gram, tau, send4, recv4,
    owner_sem, row_sem, slab_sem, sa, ra, sb, rb, spa, rpa, spb, rpb, s3, r3, st, rt, s4, r4,
):
    half = cols * CHUNKS
    me = lax.axis_index("row")
    col = lax.axis_index("col")
    left = lax.rem(me + parts - 1, parts)
    right = lax.rem(me + 1, parts)

    def others(size, mine, step):
        def body(r, _):
            step(lax.rem(mine + r, size))
            return 0

        lax.fori_loop(1, size, body, 0)

    def farthest_first(fast, size, mine, step):
        slow = size // fast
        moves = [(a, b) for a in range(slow) for b in range(fast) if a or b]
        moves.sort(key=lambda m: -(min(m[0], slow - m[0]) + min(m[1], fast - m[1])))
        for a, b in moves:
            step(lax.rem(mine // fast + a, slow) * fast + lax.rem(lax.rem(mine, fast) + b, fast))

    barrier = pltpu.get_barrier_semaphore()
    others(parts, me, lambda to: pl.semaphore_signal(
        barrier, inc=1, device_id={"row": to}, device_id_type=MESH))
    others(cols, col, lambda to: pl.semaphore_signal(
        barrier, inc=1, device_id={"col": to}, device_id_type=MESH))
    owner_copy = pltpu.make_async_copy(owner_hbm, owner_ref, owner_sem)
    owner_copy.start()
    row_copy = pltpu.make_async_copy(stored_ref, row_in, row_sem)
    row_copy.start()

    def slab_copy(b):
        return pltpu.make_async_copy(
            slab_ref.at[:, pl.ds(pl.multiple_of(b * WIDE, WIDE), WIDE)], slab_in.at[b], slab_sem.at[b]
        )

    lax.fori_loop(0, cols, lambda b, _: (slab_copy(b).start(), 0)[1], 0)

    row_copy.wait()
    low_lanes = lax.broadcasted_iota(jnp.int32, (half, LANES), 1) < BAND
    for q in range(parts // 2):
        even = row_in[pl.ds(q, half, stride=parts), :]
        odd = row_in[pl.ds(q + parts // 2, half, stride=parts), :]
        first_half = jnp.where(low_lanes, even, pltpu.roll(odd, BAND, 1))
        second_half = jnp.where(low_lanes, pltpu.roll(even, BAND, 1), odd)
        for p, mixed in ((2 * q, first_half), (2 * q + 1, second_half)):
            pieces = mixed.reshape(cols // 2, 2, CHUNKS, LANES)
            send_a[p] = pieces[:, 0]
            send_b[:, p] = pieces[:, 1]

    odd = lax.rem(col, 2) == 1

    def copy_a(to):
        return pltpu.make_async_remote_copy(
            src_ref=send_a.at[to], dst_ref=recv_a.at[me], send_sem=sa, recv_sem=ra,
            device_id={"row": to}, device_id_type=MESH,
        )

    def copy_b(i):
        return pltpu.make_async_remote_copy(
            src_ref=send_b.at[i], dst_ref=recv_b.at[col], send_sem=sb.at[i], recv_sem=rb,
            device_id={"col": 2 * i + 1}, device_id_type=MESH,
        )

    def pick_copy_a(i):
        return pltpu.make_async_remote_copy(
            src_ref=pick_a.at[i], dst_ref=from_a.at[col], send_sem=spa.at[i], recv_sem=rpa,
            device_id={"col": 2 * i}, device_id_type=MESH,
        )

    def pick_copy_b(to):
        return pltpu.make_async_remote_copy(
            src_ref=pick_b.at[to], dst_ref=from_b.at[me], send_sem=spb, recv_sem=rpb,
            device_id={"row": to}, device_id_type=MESH,
        )

    def each_other(parity, step):
        def body(r, _):
            i = lax.rem(col // 2 + r, cols // 2)

            @pl.when(2 * i + parity != col)
            def _():
                step(i)

            return 0

        lax.fori_loop(0, cols // 2, body, 0)

    def wait_for(ref, count, sem):
        taken = ref.at[pl.ds(0, count)]
        pltpu.make_async_copy(taken, taken, sem).wait()

    def copy3(to, source):
        return pltpu.make_async_remote_copy(
            src_ref=recv3.at[source], dst_ref=recv3.at[source], send_sem=s3.at[to], recv_sem=r3.at[source],
            device_id={"col": to}, device_id_type=MESH,
        )

    pl.semaphore_wait(barrier, parts + cols - 2)
    each_other(1, lambda i: copy_b(i).start())
    farthest_first(4, parts, me, lambda to: copy_a(to).start())
    recv_a[me] = send_a[me]

    @pl.when(odd)
    def _():
        recv_b[col] = send_b[col // 2]


    rows = slab_in.shape[1]

    def split_block(b, _):
        slab_copy(b).wait()

        def split_rows(i, _):
            at = pl.ds(pl.multiple_of(i * 32, 32), 32)
            high, low = split(slab_in[b, at, :])
            high_in[b, at, :] = high
            low_in[b, at, :] = low
            return 0

        return lax.fori_loop(0, rows // 32, split_rows, 0)

    lax.fori_loop(0, cols, split_block, 0)

    owner_copy.wait()
    @pl.when(odd)
    def _():
        wait_for(recv_b, cols - 1, rb)
        for g in range(GROUPS):
            pick_b[:, g] = recv_b[lax.rem(owner_ref[g], cols)]
        from_b[me] = pick_b[me]
        farthest_first(4, parts, me, lambda to: pick_copy_b(to).start())

    wait_for(recv_a, parts - 1, ra)
    for g in range(GROUPS):
        pick_a[:, g] = recv_a[owner_ref[g] // cols]
    each_other(0, lambda i: pick_copy_a(i).start())

    @pl.when(odd)
    def _():
        wait_for(from_b, parts - 1, rpb)
        for g in range(GROUPS):
            recv3[col, g] = from_b[owner_ref[g] // cols, g]

    @pl.when(jnp.logical_not(odd))
    def _():
        from_a[col] = pick_a[col // 2]
        wait_for(from_a, cols - 1, rpa)
        for g in range(GROUPS):
            recv3[col, g] = from_a[lax.rem(owner_ref[g], cols), g]

    farthest_first(2, cols, col, lambda to: copy3(to, col).start())

    lane8 = lax.broadcasted_iota(jnp.int32, (CHUNKS, LANES), 1)

    def piece_sums(product, lane, lo, hi):
        return [
            jnp.sum(
                jnp.where((lane >= BAND * par + lo) & (lane < BAND * par + hi), product, 0.0),
                axis=1, keepdims=True,
            )
            for par in range(2)
        ]

    def partial(b):
        for t, both in enumerate(spread(recv3[b])):
            spread_ref[b, t] = both
            lines = both.shape[0] // 2
            at = slice(t * PAIR, (t + 1) * PAIR)
            one = contract_lanes(both, high_in[b, :, at])
            two = contract_lanes(both[:lines], low_in[b, :, at])
            first = (b * CHUNKS + 2 * t) * SUMS
            total = one[:lines] + (one[lines:] + two)
            for n in range(rows // LANES):
                raw[n, pl.ds(pl.multiple_of(first, 2 * SUMS), lines), :] = total[:, n * LANES:(n + 1) * LANES]

    def square_sums(b):
        at = pl.ds(pl.multiple_of(b * CHUNKS, CHUNKS), CHUNKS)
        piece = recv3[b]
        squares = [jnp.zeros((CHUNKS, LANES), F32) for _ in range(2)]
        for g in range(GROUPS):
            for s in range(2):
                sums = piece_sums(piece[g] * piece[g], lane8, *segment(g, s))
                squares = [jnp.where(lane8 == 2 * g + s, sums[par], squares[par]) for par in range(2)]
        for par in range(2):
            packed[par, at, :] = squares[par]

    pair = (col // 2) * 2
    partner = pair + 1 - lax.rem(col, 2)
    chips = cols // 2

    def arrived(i):
        away = jnp.where(lax.rem(i, 2) == 1, (i + 1) // 2, chips - i // 2)
        src = lax.rem(pair + 2 * away, cols)
        copy3(src, src).wait_recv()
        copy3(src + 1, src + 1).wait_recv()
        return src

    def work(src):
        for b in (src, src + 1):
            square_sums(b)
        for b in (src, src + 1):
            partial(b)

    copy3(partner, partner).wait_recv()
    final = pair
    if chips > 1:
        work(pair)
        lax.fori_loop(1, chips - 1, lambda i, _: (work(arrived(i)), 0)[1], 0)
        final = arrived(jnp.int32(chips - 1))
    square_sums(final)
    square_sums(final + 1)
    vectors = [recv3[:, g].reshape(half, LANES) for g in range(GROUPS)]
    lane = lax.broadcasted_iota(jnp.int32, (half, LANES), 1)
    square_out[...] = jnp.concatenate([packed[0], packed[1]], axis=0).T[:2 * GROUPS, :]

    def square_copy(way, to):
        return pltpu.make_async_remote_copy(
            src_ref=square_out, dst_ref=square_in.at[way], send_sem=st.at[way], recv_sem=rt.at[way],
            device_id={"row": to}, device_id_type=MESH,
        )

    square_copies = [square_copy(0, left), square_copy(1, right)]
    for c in square_copies:
        c.start()
    partial(final)
    partial(final + 1)

    blocks = rows // LANES
    part = half // PIECES
    steps = [(n, q, par) for n in range(blocks) for q in range(PIECES) for par in range(2)]
    last = me == parts - 1
    first = me == 0

    def exchange(g, n, way, par, q):
        to = left if way == 0 else right
        at = pl.ds(q * part, part)
        return pltpu.make_async_remote_copy(
            src_ref=send4.at[g, n, way, par, at], dst_ref=recv4.at[g, n, way, par, at],
            send_sem=s4.at[g, n, way, par, q], recv_sem=r4.at[g, n, way, par, q],
            device_id={"row": to}, device_id_type=MESH,
        )

    def line(q, g, s, par):
        return pl.ds(q * part * SUMS + 4 * g + 2 * s + par, part, stride=SUMS)

    def prepare(g, n, q, par):
        tiles = pl.ds(q * part, part)
        for s in range(2):
            x = raw[n, line(q, g, s, par), :]
            for k, (pg, ps, h, t, _, _) in enumerate(PAIRS):
                if (pg, ps) == (g, s):
                    x = x - gram[k, par, tiles] * coef_ref[n, line(q, h, t, par), :]
            send4[g, n, s, par, tiles] = x
        exchange(g, n, 0, par, q).start()
        exchange(g, n, 1, par, q).start()

    def of_next(x, par):
        return jnp.where(last, pltpu.roll(x, half - 1, 0), x) if par else x

    def of_previous(x, par):
        return x if par else jnp.where(first, pltpu.roll(x, 1, 0), x)

    def next_parity(par):
        return jnp.where(last, 1 - par, par)

    def previous_parity(par):
        return jnp.where(first, 1 - par, par)

    def heads_after(g, n, q, par):
        from_ref = recv4.at[g, n, 0, next_parity(par)]
        if par == 0:
            exchange(g, n, 0, next_parity(par), q).wait_recv()
            return from_ref[q * part:(q + 1) * part]

        @pl.when(jnp.logical_not(last))
        def _():
            exchange(g, n, 0, 1, q).wait_recv()

        @pl.when(last)
        def _():
            if q == 0:
                exchange(g, n, 0, 0, 0).wait_recv()
            if q + 1 < PIECES:
                exchange(g, n, 0, 0, q + 1).wait_recv()

        def shifted():
            if q + 1 < PIECES:
                return from_ref[q * part + 1:(q + 1) * part + 1]
            return pltpu.roll(from_ref[q * part:(q + 1) * part], part - 1, 0)

        return lax.cond(last, shifted, lambda: from_ref[q * part:(q + 1) * part])

    def tails_before(g, n, q, par):
        from_ref = recv4.at[g, n, 1, previous_parity(par)]
        exchange(g, n, 1, previous_parity(par), q).wait_recv()
        if par:
            return from_ref[q * part:(q + 1) * part]

        def shifted():
            if q:
                return from_ref[q * part - 1:(q + 1) * part - 1]
            return pltpu.roll(from_ref[0:part], 1, 0)

        return lax.cond(first, shifted, lambda: from_ref[q * part:(q + 1) * part])

    def finish(g, n, q, par):
        tiles = pl.ds(q * part, part)
        after = heads_after(g, n, q, par)
        before = tails_before(g, n, q, par)
        head, tail = send4[g, n, 0, par, tiles], send4[g, n, 1, par, tiles]
        coef_ref[n, line(q, g, 0, par), :] = tau[2 * g, par, tiles] * (before + head)
        coef_ref[n, line(q, g, 1, par), :] = tau[2 * g + 1, par, tiles] * (tail + after)

    for n, q, par in steps:
        prepare(0, n, q, par)

    for k, (g, s, h, t, lo, hi) in enumerate(PAIRS):
        sums = piece_sums(vectors[g] * vectors[h], lane, lo, hi)
        for par in range(2):
            gram[k, par] = jnp.broadcast_to(sums[par], (half, LANES))

    for c in square_copies:
        c.wait()

    def turned(way):
        full = jnp.concatenate([square_in[way]] * (2 * half // (2 * GROUPS)), axis=0).T
        return [full[:half], full[half:]]

    right_squares, left_squares = turned(0), turned(1)
    at = lax.broadcasted_iota(jnp.int32, (half, 1), 0)
    for par in range(2):
        after = of_next(jnp.where(last, right_squares[1 - par], right_squares[par]), par)
        before = of_previous(jnp.where(first, left_squares[1 - par], left_squares[par]), par)
        here = packed[par]
        for g in range(GROUPS):
            head, tail = slice(2 * g, 2 * g + 1), slice(2 * g + 1, 2 * g + 2)
            own = 2.0 / (here[:, tail] + after[:, head] + 1e-06)
            prior = 2.0 / (before[:, tail] + here[:, head] + 1e-06)
            if par:
                own = jnp.where(last & (at == half - 1), 0.0, own)
            else:
                prior = jnp.where(first & (at == 0), 0.0, prior)
            tau[2 * g, par] = jnp.broadcast_to(prior, (half, LANES))
            tau[2 * g + 1, par] = jnp.broadcast_to(own, (half, LANES))

    for g in range(GROUPS):
        for n, q, par in steps:
            finish(g, n, q, par)
            if g + 1 < GROUPS:
                prepare(g + 1, n, q, par)

    wait_for(send_a, parts - 1, sa)
    each_other(1, lambda i: copy_b(i).wait_send())
    each_other(0, lambda i: pick_copy_a(i).wait_send())

    @pl.when(odd)
    def _():
        wait_for(pick_b, parts - 1, spb)

    others(cols, col, lambda to: copy3(to, col).wait_send())
    for g in range(GROUPS):
        for n, q, par in steps:
            exchange(g, n, 0, par, q).wait_send()
            exchange(g, n, 1, par, q).wait_send()


def coefficients(parts, cols, owner, stored, slab):
    rows, length = slab.shape
    half = length // LANES
    vmem, dma = pltpu.VMEM, pltpu.SemaphoreType.DMA
    blocks = rows // LANES
    piece = (cols, GROUPS, CHUNKS, LANES)
    return pl.pallas_call(
        functools.partial(coef_kernel, parts, cols),
        name="coefficients",
        out_shape=(
            jax.ShapeDtypeStruct((blocks, half * SUMS, LANES), F32),
            jax.ShapeDtypeStruct((cols, CHUNKS // 2, 4 * SUMS, PAIR), BF16),
            jax.ShapeDtypeStruct((cols, rows, WIDE), F32),
        ),
        in_specs=[
            pl.BlockSpec(memory_space=pltpu.HBM),
            pl.BlockSpec(memory_space=pltpu.HBM),
            pl.BlockSpec(memory_space=pltpu.HBM),
        ],
        out_specs=(pl.BlockSpec(memory_space=vmem),) * 3,
        scratch_shapes=[
            pltpu.SMEM((GROUPS,), jnp.int32),
            vmem(stored.shape, F32),
            vmem((cols, rows, WIDE), BF16),
            vmem((cols, rows, WIDE), BF16),
            vmem((parts, cols // 2, CHUNKS, LANES), F32),
            vmem((parts, cols // 2, CHUNKS, LANES), F32),
            vmem((cols // 2, parts, CHUNKS, LANES), F32),
            vmem((cols, parts, CHUNKS, LANES), F32),
            vmem((cols // 2, GROUPS, CHUNKS, LANES), F32),
            vmem((cols, GROUPS, CHUNKS, LANES), F32),
            vmem((parts, GROUPS, CHUNKS, LANES), F32),
            vmem((parts, GROUPS, CHUNKS, LANES), F32),
            vmem(piece, F32),
            vmem((blocks, half * SUMS, LANES), F32),
            vmem((2, half, LANES), F32),
            vmem((2 * GROUPS, 2 * half), F32),
            vmem((2, 2 * GROUPS, 2 * half), F32),
            vmem((len(PAIRS), 2, half, LANES), F32),
            vmem((2 * GROUPS, 2, half, LANES), F32),
            vmem((GROUPS, blocks, 2, 2, half, LANES), F32),
            vmem((GROUPS, blocks, 2, 2, half, LANES), F32),
            dma, dma, dma((cols,)),
            dma, dma, dma((cols // 2,)), dma,
            dma((cols // 2,)), dma, dma, dma,
            dma((cols,)), dma((cols,)),
            dma((2,)), dma((2,)),
            dma((GROUPS, blocks, 2, 2, PIECES)), dma((GROUPS, blocks, 2, 2, PIECES)),
        ],
        compiler_params=pltpu.CompilerParams(
            has_side_effects=True, collective_id=0, vmem_limit_bytes=40 * 1024 * 1024
        ),
    )(*(pltpu.with_memory_space_constraint(x, pltpu.HBM) for x in (owner, stored, slab)))


def update_kernel(cols, coef_ref, spread_ref, slab_ref, out_ref, ready, sem):
    slots = ready.shape[0]

    def copy(b):
        slot = lax.rem(b, slots)
        at = pl.ds(pl.multiple_of(b * WIDE, WIDE), WIDE)
        return pltpu.make_async_copy(ready.at[slot], out_ref.at[:, at], sem.at[slot])

    def block(b):
        lines = CHUNKS * SUMS
        at = pl.ds(pl.multiple_of(b * lines, lines), lines)
        high, low = split(jnp.concatenate([coef_ref[n, at, :] for n in range(coef_ref.shape[0])], axis=1))
        stack = []
        for t in range(CHUNKS // 2):
            at = slice(t * 2 * SUMS, (t + 1) * 2 * SUMS)
            stack += [high[at], high[at], low[at], low[at]]
        turned = jnp.concatenate(stack, axis=0).T
        for t in range(CHUNKS // 2):
            both = spread_ref[b, t]
            depth = 2 * both.shape[0]
            change = jnp.dot(
                turned[:, t * depth:(t + 1) * depth], jnp.concatenate([both, both], axis=0),
                preferred_element_type=F32,
            )
            at = slice(t * PAIR, (t + 1) * PAIR)
            ready[lax.rem(b, slots), :, at] = slab_ref[b, :, at] - change

    def two(i, _):
        @pl.when(i >= slots // 2)
        def _():
            copy(2 * i - slots).wait()
            copy(2 * i + 1 - slots).wait()

        block(2 * i)
        copy(2 * i).start()
        block(2 * i + 1)
        copy(2 * i + 1).start()
        return 0

    lax.fori_loop(0, cols // 2, two, 0)
    lax.fori_loop(max(cols - slots, 0), cols, lambda b, _: (copy(b).wait(), 0)[1], 0)


def update(cols, coef, wide, slab_in):
    blocks, rows, length = slab_in.shape
    return pl.pallas_call(
        functools.partial(update_kernel, cols),
        name="update",
        out_shape=jax.ShapeDtypeStruct((rows, blocks * length), F32),
        in_specs=[pl.BlockSpec(memory_space=pltpu.VMEM)] * 3,
        out_specs=pl.BlockSpec(memory_space=pltpu.HBM),
        scratch_shapes=[pltpu.VMEM((4, rows, length), F32), pltpu.SemaphoreType.DMA((4,))],
        compiler_params=pltpu.CompilerParams(vmem_limit_bytes=24 * 1024 * 1024),
    )(coef, wide, slab_in)


def shards(parts, cols, slab, stored, owner):
    coef, wide, slab_in = coefficients(parts, cols, owner, stored.reshape(-1, LANES), slab)
    return update(cols, coef, wide, slab_in)


def solution(mesh):
    placed = (P("col", "row"), P(("row", "col"), None), P())
    body = functools.partial(shards, mesh.shape["row"], mesh.shape["col"])
    return jax.shard_map(
        body, mesh=mesh, in_specs=placed, out_specs=P("col", "row"), check_vma=False
    )
```

```python
import functools

import jax
import jax.numpy as jnp
from jax import lax
from jax.experimental import pallas as pl
from jax.experimental.pallas import tpu as pltpu
from jax.sharding import PartitionSpec as P

BAND = 64
GROUPS = 4
LANES = 128
CHUNKS = 8
WIDE = CHUNKS * LANES
SUMS = 4 * GROUPS
PAIR = 2 * LANES
PIECES = 2
MESH = pl.DeviceIdType.MESH
F32 = jnp.float32
BF16 = jnp.bfloat16


def offset_of(group):
    return 1 + (37 * group + 11) % 63


def segment(group, side):
    return (0, offset_of(group)) if side == 0 else (offset_of(group), BAND)


PAIRS = []
for _g in range(GROUPS):
    for _s in range(2):
        for _h in range(_g):
            for _t in range(2):
                _lo = max(segment(_g, _s)[0], segment(_h, _t)[0])
                _hi = min(segment(_g, _s)[1], segment(_h, _t)[1])
                if _lo < _hi:
                    PAIRS.append((_g, _s, _h, _t, _lo, _hi))


def split(x):
    high = x.astype(BF16)
    return high, (x - high.astype(F32)).astype(BF16)


def spread(vectors):
    shape = (SUMS, LANES)
    lane = lax.broadcasted_iota(jnp.int32, shape, 1)
    line = lax.broadcasted_iota(jnp.int32, shape, 0)
    group = line // 4
    at = lane - BAND * lax.rem(line, 2)
    keep = jnp.zeros(shape, jnp.bool_)
    for g in range(GROUPS):
        for s in range(2):
            lo, hi = segment(g, s)
            keep = keep | ((line // 2 == 2 * g + s) & (at >= lo) & (at < hi))
    none = jnp.zeros(shape, BF16)
    halves = []
    for i in range(CHUNKS):
        rows = [jnp.broadcast_to(vectors[g][i:i + 1, :], shape) for g in range(GROUPS)]
        own = rows[0]
        for g in range(1, GROUPS):
            own = jnp.where(group == g, rows[g], own)
        halves.append(split(jnp.where(keep, own, 0.0)))
    pairs = []
    for i in range(0, CHUNKS, 2):
        first, second = halves[i], halves[i + 1]
        lines = []
        for term in range(2):
            lines.append(jnp.concatenate([first[term], none], axis=1))
            lines.append(jnp.concatenate([none, second[term]], axis=1))
        pairs.append(jnp.concatenate(lines, axis=0))
    return pairs


def contract_lanes(a, b):
    return lax.dot_general(a, b, (((1,), (1,)), ((), ())), preferred_element_type=F32)


def coef_kernel(
    parts, cols, owner_hbm, stored_ref, slab_ref, coef_ref, spread_ref, slab_in,
    owner_ref, row_in, high_in, low_in, send_a, recv_a, send_b, recv_b, pick_a, from_a, pick_b, from_b, recv3,
    raw, packed, square_out, square_in, gram, tau, send4, recv4,
    owner_sem, row_sem, slab_sem, sa, ra, sb, rb, spa, rpa, spb, rpb, s3, r3, st, rt, s4, r4,
):
    half = cols * CHUNKS
    me = lax.axis_index("row")
    col = lax.axis_index("col")
    left = lax.rem(me + parts - 1, parts)
    right = lax.rem(me + 1, parts)

    def others(size, mine, step):
        def body(r, _):
            step(lax.rem(mine + r, size))
            return 0

        lax.fori_loop(1, size, body, 0)

    def farthest_first(fast, size, mine, step):
        slow = size // fast
        moves = [(a, b) for a in range(slow) for b in range(fast) if a or b]
        moves.sort(key=lambda m: -(min(m[0], slow - m[0]) + min(m[1], fast - m[1])))
        for a, b in moves:
            step(lax.rem(mine // fast + a, slow) * fast + lax.rem(lax.rem(mine, fast) + b, fast))

    barrier = pltpu.get_barrier_semaphore()
    others(parts, me, lambda to: pl.semaphore_signal(
        barrier, inc=1, device_id={"row": to}, device_id_type=MESH))
    others(cols, col, lambda to: pl.semaphore_signal(
        barrier, inc=1, device_id={"col": to}, device_id_type=MESH))
    owner_copy = pltpu.make_async_copy(owner_hbm, owner_ref, owner_sem)
    owner_copy.start()
    row_copy = pltpu.make_async_copy(stored_ref, row_in, row_sem)
    row_copy.start()

    def slab_copy(b):
        return pltpu.make_async_copy(
            slab_ref.at[:, pl.ds(pl.multiple_of(b * WIDE, WIDE), WIDE)], slab_in.at[b], slab_sem.at[b]
        )

    lax.fori_loop(0, cols, lambda b, _: (slab_copy(b).start(), 0)[1], 0)

    row_copy.wait()
    low_lanes = lax.broadcasted_iota(jnp.int32, (half, LANES), 1) < BAND
    for q in range(parts // 2):
        even = row_in[pl.ds(q, half, stride=parts), :]
        odd = row_in[pl.ds(q + parts // 2, half, stride=parts), :]
        first_half = jnp.where(low_lanes, even, pltpu.roll(odd, BAND, 1))
        second_half = jnp.where(low_lanes, pltpu.roll(even, BAND, 1), odd)
        for p, mixed in ((2 * q, first_half), (2 * q + 1, second_half)):
            pieces = mixed.reshape(cols // 2, 2, CHUNKS, LANES)
            send_a[p] = pieces[:, 0]
            send_b[:, p] = pieces[:, 1]

    odd = lax.rem(col, 2) == 1

    def copy_a(to):
        return pltpu.make_async_remote_copy(
            src_ref=send_a.at[to], dst_ref=recv_a.at[me], send_sem=sa, recv_sem=ra,
            device_id={"row": to}, device_id_type=MESH,
        )

    def copy_b(i):
        return pltpu.make_async_remote_copy(
            src_ref=send_b.at[i], dst_ref=recv_b.at[col], send_sem=sb.at[i], recv_sem=rb,
            device_id={"col": 2 * i + 1}, device_id_type=MESH,
        )

    def pick_copy_a(i):
        return pltpu.make_async_remote_copy(
            src_ref=pick_a.at[i], dst_ref=from_a.at[col], send_sem=spa.at[i], recv_sem=rpa,
            device_id={"col": 2 * i}, device_id_type=MESH,
        )

    def pick_copy_b(to):
        return pltpu.make_async_remote_copy(
            src_ref=pick_b.at[to], dst_ref=from_b.at[me], send_sem=spb, recv_sem=rpb,
            device_id={"row": to}, device_id_type=MESH,
        )

    def each_other(parity, step):
        def body(r, _):
            i = lax.rem(col // 2 + r, cols // 2)

            @pl.when(2 * i + parity != col)
            def _():
                step(i)

            return 0

        lax.fori_loop(0, cols // 2, body, 0)

    def wait_for(ref, count, sem):
        taken = ref.at[pl.ds(0, count)]
        pltpu.make_async_copy(taken, taken, sem).wait()

    def copy3(to, source):
        return pltpu.make_async_remote_copy(
            src_ref=recv3.at[source], dst_ref=recv3.at[source], send_sem=s3.at[to], recv_sem=r3.at[source],
            device_id={"col": to}, device_id_type=MESH,
        )

    pl.semaphore_wait(barrier, parts + cols - 2)
    farthest_first(4, parts, me, lambda to: copy_a(to).start())
    each_other(1, lambda i: copy_b(i).start())
    recv_a[me] = send_a[me]

    @pl.when(odd)
    def _():
        recv_b[col] = send_b[col // 2]


    rows = slab_in.shape[1]

    def split_block(b, _):
        slab_copy(b).wait()

        def split_rows(i, _):
            at = pl.ds(pl.multiple_of(i * 32, 32), 32)
            high, low = split(slab_in[b, at, :])
            high_in[b, at, :] = high
            low_in[b, at, :] = low
            return 0

        return lax.fori_loop(0, rows // 32, split_rows, 0)

    lax.fori_loop(0, cols, split_block, 0)

    owner_copy.wait()
    @pl.when(odd)
    def _():
        wait_for(recv_b, cols - 1, rb)
        for g in range(GROUPS):
            pick_b[:, g] = recv_b[lax.rem(owner_ref[g], cols)]
        from_b[me] = pick_b[me]
        farthest_first(4, parts, me, lambda to: pick_copy_b(to).start())

    wait_for(recv_a, parts - 1, ra)
    for g in range(GROUPS):
        pick_a[:, g] = recv_a[owner_ref[g] // cols]
    each_other(0, lambda i: pick_copy_a(i).start())

    @pl.when(odd)
    def _():
        wait_for(from_b, parts - 1, rpb)
        for g in range(GROUPS):
            recv3[col, g] = from_b[owner_ref[g] // cols, g]

    @pl.when(jnp.logical_not(odd))
    def _():
        from_a[col] = pick_a[col // 2]
        wait_for(from_a, cols - 1, rpa)
        for g in range(GROUPS):
            recv3[col, g] = from_a[lax.rem(owner_ref[g], cols), g]

    farthest_first(2, cols, col, lambda to: copy3(to, col).start())

    lane8 = lax.broadcasted_iota(jnp.int32, (CHUNKS, LANES), 1)

    def piece_sums(product, lane, lo, hi):
        return [
            jnp.sum(
                jnp.where((lane >= BAND * par + lo) & (lane < BAND * par + hi), product, 0.0),
                axis=1, keepdims=True,
            )
            for par in range(2)
        ]

    def partial(b):
        for t, both in enumerate(spread(recv3[b])):
            spread_ref[b, t] = both
            lines = both.shape[0] // 2
            at = slice(t * PAIR, (t + 1) * PAIR)
            one = contract_lanes(both, high_in[b, :, at])
            two = contract_lanes(both[:lines], low_in[b, :, at])
            first = (b * CHUNKS + 2 * t) * SUMS
            total = one[:lines] + (one[lines:] + two)
            for n in range(rows // LANES):
                raw[n, pl.ds(pl.multiple_of(first, 2 * SUMS), lines), :] = total[:, n * LANES:(n + 1) * LANES]

    def square_sums(b):
        at = pl.ds(pl.multiple_of(b * CHUNKS, CHUNKS), CHUNKS)
        piece = recv3[b]
        squares = [jnp.zeros((CHUNKS, LANES), F32) for _ in range(2)]
        for g in range(GROUPS):
            for s in range(2):
                sums = piece_sums(piece[g] * piece[g], lane8, *segment(g, s))
                squares = [jnp.where(lane8 == 2 * g + s, sums[par], squares[par]) for par in range(2)]
        for par in range(2):
            packed[par, at, :] = squares[par]

    pair = (col // 2) * 2
    partner = pair + 1 - lax.rem(col, 2)
    chips = cols // 2

    def arrived(i):
        away = jnp.where(lax.rem(i, 2) == 1, (i + 1) // 2, chips - i // 2)
        src = lax.rem(pair + 2 * away, cols)
        copy3(src, src).wait_recv()
        copy3(src + 1, src + 1).wait_recv()
        return src

    def work(src):
        for b in (src, src + 1):
            square_sums(b)
        for b in (src, src + 1):
            partial(b)

    copy3(partner, partner).wait_recv()
    final = pair
    if chips > 1:
        work(pair)
        lax.fori_loop(1, chips - 1, lambda i, _: (work(arrived(i)), 0)[1], 0)
        final = arrived(jnp.int32(chips - 1))
    square_sums(final)
    square_sums(final + 1)
    vectors = [recv3[:, g].reshape(half, LANES) for g in range(GROUPS)]
    lane = lax.broadcasted_iota(jnp.int32, (half, LANES), 1)
    square_out[...] = jnp.concatenate([packed[0], packed[1]], axis=0).T[:2 * GROUPS, :]

    def square_copy(way, to):
        return pltpu.make_async_remote_copy(
            src_ref=square_out, dst_ref=square_in.at[way], send_sem=st.at[way], recv_sem=rt.at[way],
            device_id={"row": to}, device_id_type=MESH,
        )

    square_copies = [square_copy(0, left), square_copy(1, right)]
    for c in square_copies:
        c.start()
    partial(final)
    partial(final + 1)

    blocks = rows // LANES
    part = half // PIECES
    steps = [(n, q, par) for n in range(blocks) for q in range(PIECES) for par in range(2)]
    last = me == parts - 1
    first = me == 0

    def exchange(g, n, way, par, q):
        to = left if way == 0 else right
        at = pl.ds(q * part, part)
        return pltpu.make_async_remote_copy(
            src_ref=send4.at[g, n, way, par, at], dst_ref=recv4.at[g, n, way, par, at],
            send_sem=s4.at[g, n, way, par, q], recv_sem=r4.at[g, n, way, par, q],
            device_id={"row": to}, device_id_type=MESH,
        )

    def line(q, g, s, par):
        return pl.ds(q * part * SUMS + 4 * g + 2 * s + par, part, stride=SUMS)

    def prepare(g, n, q, par):
        tiles = pl.ds(q * part, part)
        for s in range(2):
            x = raw[n, line(q, g, s, par), :]
            for k, (pg, ps, h, t, _, _) in enumerate(PAIRS):
                if (pg, ps) == (g, s):
                    x = x - gram[k, par, tiles] * coef_ref[n, line(q, h, t, par), :]
            send4[g, n, s, par, tiles] = x
        exchange(g, n, 0, par, q).start()
        exchange(g, n, 1, par, q).start()

    def of_next(x, par):
        return jnp.where(last, pltpu.roll(x, half - 1, 0), x) if par else x

    def of_previous(x, par):
        return x if par else jnp.where(first, pltpu.roll(x, 1, 0), x)

    def next_parity(par):
        return jnp.where(last, 1 - par, par)

    def previous_parity(par):
        return jnp.where(first, 1 - par, par)

    def heads_after(g, n, q, par):
        from_ref = recv4.at[g, n, 0, next_parity(par)]
        if par == 0:
            exchange(g, n, 0, next_parity(par), q).wait_recv()
            return from_ref[q * part:(q + 1) * part]

        @pl.when(jnp.logical_not(last))
        def _():
            exchange(g, n, 0, 1, q).wait_recv()

        @pl.when(last)
        def _():
            if q == 0:
                exchange(g, n, 0, 0, 0).wait_recv()
            if q + 1 < PIECES:
                exchange(g, n, 0, 0, q + 1).wait_recv()

        def shifted():
            if q + 1 < PIECES:
                return from_ref[q * part + 1:(q + 1) * part + 1]
            return pltpu.roll(from_ref[q * part:(q + 1) * part], part - 1, 0)

        return lax.cond(last, shifted, lambda: from_ref[q * part:(q + 1) * part])

    def tails_before(g, n, q, par):
        from_ref = recv4.at[g, n, 1, previous_parity(par)]
        exchange(g, n, 1, previous_parity(par), q).wait_recv()
        if par:
            return from_ref[q * part:(q + 1) * part]

        def shifted():
            if q:
                return from_ref[q * part - 1:(q + 1) * part - 1]
            return pltpu.roll(from_ref[0:part], 1, 0)

        return lax.cond(first, shifted, lambda: from_ref[q * part:(q + 1) * part])

    def finish(g, n, q, par):
        tiles = pl.ds(q * part, part)
        after = heads_after(g, n, q, par)
        before = tails_before(g, n, q, par)
        head, tail = send4[g, n, 0, par, tiles], send4[g, n, 1, par, tiles]
        coef_ref[n, line(q, g, 0, par), :] = tau[2 * g, par, tiles] * (before + head)
        coef_ref[n, line(q, g, 1, par), :] = tau[2 * g + 1, par, tiles] * (tail + after)

    for n, q, par in steps:
        prepare(0, n, q, par)

    for k, (g, s, h, t, lo, hi) in enumerate(PAIRS):
        sums = piece_sums(vectors[g] * vectors[h], lane, lo, hi)
        for par in range(2):
            gram[k, par] = jnp.broadcast_to(sums[par], (half, LANES))

    for c in square_copies:
        c.wait()

    def turned(way):
        full = jnp.concatenate([square_in[way]] * (2 * half // (2 * GROUPS)), axis=0).T
        return [full[:half], full[half:]]

    right_squares, left_squares = turned(0), turned(1)
    at = lax.broadcasted_iota(jnp.int32, (half, 1), 0)
    for par in range(2):
        after = of_next(jnp.where(last, right_squares[1 - par], right_squares[par]), par)
        before = of_previous(jnp.where(first, left_squares[1 - par], left_squares[par]), par)
        here = packed[par]
        for g in range(GROUPS):
            head, tail = slice(2 * g, 2 * g + 1), slice(2 * g + 1, 2 * g + 2)
            own = 2.0 / (here[:, tail] + after[:, head] + 1e-06)
            prior = 2.0 / (before[:, tail] + here[:, head] + 1e-06)
            if par:
                own = jnp.where(last & (at == half - 1), 0.0, own)
            else:
                prior = jnp.where(first & (at == 0), 0.0, prior)
            tau[2 * g, par] = jnp.broadcast_to(prior, (half, LANES))
            tau[2 * g + 1, par] = jnp.broadcast_to(own, (half, LANES))

    for g in range(GROUPS):
        for n, q, par in steps:
            finish(g, n, q, par)
            if g + 1 < GROUPS:
                prepare(g + 1, n, q, par)

    wait_for(send_a, parts - 1, sa)
    each_other(1, lambda i: copy_b(i).wait_send())
    each_other(0, lambda i: pick_copy_a(i).wait_send())

    @pl.when(odd)
    def _():
        wait_for(pick_b, parts - 1, spb)

    others(cols, col, lambda to: copy3(to, col).wait_send())
    for g in range(GROUPS):
        for n, q, par in steps:
            exchange(g, n, 0, par, q).wait_send()
            exchange(g, n, 1, par, q).wait_send()


def coefficients(parts, cols, owner, stored, slab):
    rows, length = slab.shape
    half = length // LANES
    vmem, dma = pltpu.VMEM, pltpu.SemaphoreType.DMA
    blocks = rows // LANES
    piece = (cols, GROUPS, CHUNKS, LANES)
    return pl.pallas_call(
        functools.partial(coef_kernel, parts, cols),
        name="coefficients",
        out_shape=(
            jax.ShapeDtypeStruct((blocks, half * SUMS, LANES), F32),
            jax.ShapeDtypeStruct((cols, CHUNKS // 2, 4 * SUMS, PAIR), BF16),
            jax.ShapeDtypeStruct((cols, rows, WIDE), F32),
        ),
        in_specs=[
            pl.BlockSpec(memory_space=pltpu.HBM),
            pl.BlockSpec(memory_space=pltpu.HBM),
            pl.BlockSpec(memory_space=pltpu.HBM),
        ],
        out_specs=(pl.BlockSpec(memory_space=vmem),) * 3,
        scratch_shapes=[
            pltpu.SMEM((GROUPS,), jnp.int32),
            vmem(stored.shape, F32),
            vmem((cols, rows, WIDE), BF16),
            vmem((cols, rows, WIDE), BF16),
            vmem((parts, cols // 2, CHUNKS, LANES), F32),
            vmem((parts, cols // 2, CHUNKS, LANES), F32),
            vmem((cols // 2, parts, CHUNKS, LANES), F32),
            vmem((cols, parts, CHUNKS, LANES), F32),
            vmem((cols // 2, GROUPS, CHUNKS, LANES), F32),
            vmem((cols, GROUPS, CHUNKS, LANES), F32),
            vmem((parts, GROUPS, CHUNKS, LANES), F32),
            vmem((parts, GROUPS, CHUNKS, LANES), F32),
            vmem(piece, F32),
            vmem((blocks, half * SUMS, LANES), F32),
            vmem((2, half, LANES), F32),
            vmem((2 * GROUPS, 2 * half), F32),
            vmem((2, 2 * GROUPS, 2 * half), F32),
            vmem((len(PAIRS), 2, half, LANES), F32),
            vmem((2 * GROUPS, 2, half, LANES), F32),
            vmem((GROUPS, blocks, 2, 2, half, LANES), F32),
            vmem((GROUPS, blocks, 2, 2, half, LANES), F32),
            dma, dma, dma((cols,)),
            dma, dma, dma((cols // 2,)), dma,
            dma((cols // 2,)), dma, dma, dma,
            dma((cols,)), dma((cols,)),
            dma((2,)), dma((2,)),
            dma((GROUPS, blocks, 2, 2, PIECES)), dma((GROUPS, blocks, 2, 2, PIECES)),
        ],
        compiler_params=pltpu.CompilerParams(
            has_side_effects=True, collective_id=0, vmem_limit_bytes=40 * 1024 * 1024
        ),
    )(*(pltpu.with_memory_space_constraint(x, pltpu.HBM) for x in (owner, stored, slab)))


def update_kernel(cols, coef_ref, spread_ref, slab_ref, out_ref, ready, sem):
    slots = ready.shape[0]

    def copy(b):
        slot = lax.rem(b, slots)
        at = pl.ds(pl.multiple_of(b * WIDE, WIDE), WIDE)
        return pltpu.make_async_copy(ready.at[slot], out_ref.at[:, at], sem.at[slot])

    def block(b):
        lines = CHUNKS * SUMS
        at = pl.ds(pl.multiple_of(b * lines, lines), lines)
        high, low = split(jnp.concatenate([coef_ref[n, at, :] for n in range(coef_ref.shape[0])], axis=1))
        stack = []
        for t in range(CHUNKS // 2):
            at = slice(t * 2 * SUMS, (t + 1) * 2 * SUMS)
            stack += [high[at], high[at], low[at], low[at]]
        turned = jnp.concatenate(stack, axis=0).T
        for t in range(CHUNKS // 2):
            both = spread_ref[b, t]
            depth = 2 * both.shape[0]
            change = jnp.dot(
                turned[:, t * depth:(t + 1) * depth], jnp.concatenate([both, both], axis=0),
                preferred_element_type=F32,
            )
            at = slice(t * PAIR, (t + 1) * PAIR)
            ready[lax.rem(b, slots), :, at] = slab_ref[b, :, at] - change

    def two(i, _):
        @pl.when(i >= slots // 2)
        def _():
            copy(2 * i - slots).wait()
            copy(2 * i + 1 - slots).wait()

        block(2 * i)
        copy(2 * i).start()
        block(2 * i + 1)
        copy(2 * i + 1).start()
        return 0

    lax.fori_loop(0, cols // 2, two, 0)
    lax.fori_loop(max(cols - slots, 0), cols, lambda b, _: (copy(b).wait(), 0)[1], 0)


def update(cols, coef, wide, slab_in):
    blocks, rows, length = slab_in.shape
    return pl.pallas_call(
        functools.partial(update_kernel, cols),
        name="update",
        out_shape=jax.ShapeDtypeStruct((rows, blocks * length), F32),
        in_specs=[pl.BlockSpec(memory_space=pltpu.VMEM)] * 3,
        out_specs=pl.BlockSpec(memory_space=pltpu.HBM),
        scratch_shapes=[pltpu.VMEM((4, rows, length), F32), pltpu.SemaphoreType.DMA((4,))],
        compiler_params=pltpu.CompilerParams(vmem_limit_bytes=24 * 1024 * 1024),
    )(coef, wide, slab_in)


def shards(parts, cols, slab, stored, owner):
    coef, wide, slab_in = coefficients(parts, cols, owner, stored.reshape(-1, LANES), slab)
    return update(cols, coef, wide, slab_in)


def solution(mesh):
    placed = (P("col", "row"), P(("row", "col"), None), P())
    body = functools.partial(shards, mesh.shape["row"], mesh.shape["col"])
    return jax.shard_map(
        body, mesh=mesh, in_specs=placed, out_specs=P("col", "row"), check_vma=False
    )
```

```python
import functools

import jax
import jax.numpy as jnp
from jax import lax
from jax.experimental import pallas as pl
from jax.experimental.pallas import tpu as pltpu
from jax.sharding import PartitionSpec as P

BAND = 64
GROUPS = 4
LANES = 128
CHUNKS = 8
WIDE = CHUNKS * LANES
SUMS = 4 * GROUPS
PAIR = 2 * LANES
OUT_CUTS = 2
PIECES = 2
MESH = pl.DeviceIdType.MESH
F32 = jnp.float32
BF16 = jnp.bfloat16


def offset_of(group):
    return 1 + (37 * group + 11) % 63


def segment(group, side):
    return (0, offset_of(group)) if side == 0 else (offset_of(group), BAND)


PAIRS = []
for _g in range(GROUPS):
    for _s in range(2):
        for _h in range(_g):
            for _t in range(2):
                _lo = max(segment(_g, _s)[0], segment(_h, _t)[0])
                _hi = min(segment(_g, _s)[1], segment(_h, _t)[1])
                if _lo < _hi:
                    PAIRS.append((_g, _s, _h, _t, _lo, _hi))


def split(x):
    high = x.astype(BF16)
    return high, (x - high.astype(F32)).astype(BF16)


def spread(vectors):
    shape = (SUMS, LANES)
    lane = lax.broadcasted_iota(jnp.int32, shape, 1)
    line = lax.broadcasted_iota(jnp.int32, shape, 0)
    group = line // 4
    at = lane - BAND * lax.rem(line, 2)
    keep = jnp.zeros(shape, jnp.bool_)
    for g in range(GROUPS):
        for s in range(2):
            lo, hi = segment(g, s)
            keep = keep | ((line // 2 == 2 * g + s) & (at >= lo) & (at < hi))
    none = jnp.zeros(shape, BF16)
    halves = []
    for i in range(CHUNKS):
        rows = [jnp.broadcast_to(vectors[g][i:i + 1, :], shape) for g in range(GROUPS)]
        own = rows[0]
        for g in range(1, GROUPS):
            own = jnp.where(group == g, rows[g], own)
        halves.append(split(jnp.where(keep, own, 0.0)))
    pairs = []
    for i in range(0, CHUNKS, 2):
        first, second = halves[i], halves[i + 1]
        lines = []
        for term in range(2):
            lines.append(jnp.concatenate([first[term], none], axis=1))
            lines.append(jnp.concatenate([none, second[term]], axis=1))
        pairs.append(jnp.concatenate(lines, axis=0))
    return pairs


def contract_lanes(a, b):
    return lax.dot_general(a, b, (((1,), (1,)), ((), ())), preferred_element_type=F32)


def coef_kernel(
    parts, cols, owner_hbm, stored_ref, slab_ref, coef_ref, spread_ref, slab_in,
    owner_ref, row_in, high_in, low_in, send_a, recv_a, send_b, recv_b, pick_a, from_a, pick_b, from_b, recv3,
    raw, packed, square_out, square_in, gram, tau, send4, recv4,
    owner_sem, row_sem, slab_sem, sa, ra, sb, rb, spa, rpa, spb, rpb, s3, r3, st, rt, s4, r4,
):
    half = cols * CHUNKS
    me = lax.axis_index("row")
    col = lax.axis_index("col")
    left = lax.rem(me + parts - 1, parts)
    right = lax.rem(me + 1, parts)

    def others(size, mine, step):
        def body(r, _):
            step(lax.rem(mine + r, size))
            return 0

        lax.fori_loop(1, size, body, 0)

    def farthest_first(fast, size, mine, step):
        slow = size // fast
        moves = [(a, b) for a in range(slow) for b in range(fast) if a or b]
        moves.sort(key=lambda m: -(min(m[0], slow - m[0]) + min(m[1], fast - m[1])))
        for a, b in moves:
            step(lax.rem(mine // fast + a, slow) * fast + lax.rem(lax.rem(mine, fast) + b, fast))

    barrier = pltpu.get_barrier_semaphore()
    others(parts, me, lambda to: pl.semaphore_signal(
        barrier, inc=1, device_id={"row": to}, device_id_type=MESH))
    others(cols, col, lambda to: pl.semaphore_signal(
        barrier, inc=1, device_id={"col": to}, device_id_type=MESH))
    owner_copy = pltpu.make_async_copy(owner_hbm, owner_ref, owner_sem)
    owner_copy.start()
    row_copy = pltpu.make_async_copy(stored_ref, row_in, row_sem)
    row_copy.start()

    def slab_copy(b):
        return pltpu.make_async_copy(
            slab_ref.at[:, pl.ds(pl.multiple_of(b * WIDE, WIDE), WIDE)], slab_in.at[b], slab_sem.at[b]
        )

    lax.fori_loop(0, cols, lambda b, _: (slab_copy(b).start(), 0)[1], 0)

    row_copy.wait()
    low_lanes = lax.broadcasted_iota(jnp.int32, (half, LANES), 1) < BAND
    for q in range(parts // 2):
        even = row_in[pl.ds(q, half, stride=parts), :]
        odd = row_in[pl.ds(q + parts // 2, half, stride=parts), :]
        first_half = jnp.where(low_lanes, even, pltpu.roll(odd, BAND, 1))
        second_half = jnp.where(low_lanes, pltpu.roll(even, BAND, 1), odd)
        for p, mixed in ((2 * q, first_half), (2 * q + 1, second_half)):
            pieces = mixed.reshape(cols // 2, 2, CHUNKS, LANES)
            send_a[p] = pieces[:, 0]
            send_b[:, p] = pieces[:, 1]

    odd = lax.rem(col, 2) == 1

    def copy_a(to):
        return pltpu.make_async_remote_copy(
            src_ref=send_a.at[to], dst_ref=recv_a.at[me], send_sem=sa, recv_sem=ra,
            device_id={"row": to}, device_id_type=MESH,
        )

    def copy_b(i):
        return pltpu.make_async_remote_copy(
            src_ref=send_b.at[i], dst_ref=recv_b.at[col], send_sem=sb.at[i], recv_sem=rb,
            device_id={"col": 2 * i + 1}, device_id_type=MESH,
        )

    def pick_copy_a(i):
        return pltpu.make_async_remote_copy(
            src_ref=pick_a.at[i], dst_ref=from_a.at[col], send_sem=spa.at[i], recv_sem=rpa,
            device_id={"col": 2 * i}, device_id_type=MESH,
        )

    def pick_copy_b(to):
        return pltpu.make_async_remote_copy(
            src_ref=pick_b.at[to], dst_ref=from_b.at[me], send_sem=spb, recv_sem=rpb,
            device_id={"row": to}, device_id_type=MESH,
        )

    def each_other(parity, step):
        chips = cols // 2
        for r in sorted(range(chips), key=lambda r: -min(r, chips - r)):
            i = lax.rem(col // 2 + r, chips)
            if r:
                step(i)
            else:
                pl.when(2 * i + parity != col)(functools.partial(step, i))

    def wait_for(ref, count, sem):
        taken = ref.at[pl.ds(0, count)]
        pltpu.make_async_copy(taken, taken, sem).wait()

    def copy3(to, source):
        return pltpu.make_async_remote_copy(
            src_ref=recv3.at[source], dst_ref=recv3.at[source], send_sem=s3.at[to], recv_sem=r3.at[source],
            device_id={"col": to}, device_id_type=MESH,
        )

    pl.semaphore_wait(barrier, parts + cols - 2)
    each_other(1, lambda i: copy_b(i).start())
    farthest_first(4, parts, me, lambda to: copy_a(to).start())
    recv_a[me] = send_a[me]

    @pl.when(odd)
    def _():
        recv_b[col] = send_b[col // 2]


    rows = slab_in.shape[1]

    def split_block(b, _):
        slab_copy(b).wait()

        def split_rows(i, _):
            at = pl.ds(pl.multiple_of(i * 32, 32), 32)
            high, low = split(slab_in[b, at, :])
            high_in[b, at, :] = high
            low_in[b, at, :] = low
            return 0

        return lax.fori_loop(0, rows // 32, split_rows, 0)

    lax.fori_loop(0, cols, split_block, 0)

    owner_copy.wait()
    @pl.when(odd)
    def _():
        wait_for(recv_b, cols - 1, rb)
        for g in range(GROUPS):
            pick_b[:, g] = recv_b[lax.rem(owner_ref[g], cols)]
        from_b[me] = pick_b[me]
        farthest_first(4, parts, me, lambda to: pick_copy_b(to).start())

    wait_for(recv_a, parts - 1, ra)
    for g in range(GROUPS):
        pick_a[:, g] = recv_a[owner_ref[g] // cols]
    each_other(0, lambda i: pick_copy_a(i).start())

    @pl.when(odd)
    def _():
        wait_for(from_b, parts - 1, rpb)
        for g in range(GROUPS):
            recv3[col, g] = from_b[owner_ref[g] // cols, g]

    @pl.when(jnp.logical_not(odd))
    def _():
        from_a[col] = pick_a[col // 2]
        wait_for(from_a, cols - 1, rpa)
        for g in range(GROUPS):
            recv3[col, g] = from_a[lax.rem(owner_ref[g], cols), g]

    farthest_first(2, cols, col, lambda to: copy3(to, col).start())

    lane8 = lax.broadcasted_iota(jnp.int32, (CHUNKS, LANES), 1)

    def piece_sums(product, lane, lo, hi):
        return [
            jnp.sum(
                jnp.where((lane >= BAND * par + lo) & (lane < BAND * par + hi), product, 0.0),
                axis=1, keepdims=True,
            )
            for par in range(2)
        ]

    def partial(b):
        for t, both in enumerate(spread(recv3[b])):
            spread_ref[b, t] = both
            lines = both.shape[0] // 2
            at = slice(t * PAIR, (t + 1) * PAIR)
            one = contract_lanes(both, high_in[b, :, at])
            two = contract_lanes(both[:lines], low_in[b, :, at])
            first = (b * CHUNKS + 2 * t) * SUMS
            total = one[:lines] + (one[lines:] + two)
            for n in range(rows // LANES):
                raw[n, pl.ds(pl.multiple_of(first, 2 * SUMS), lines), :] = total[:, n * LANES:(n + 1) * LANES]

    def square_sums(b):
        at = pl.ds(pl.multiple_of(b * CHUNKS, CHUNKS), CHUNKS)
        piece = recv3[b]
        squares = [jnp.zeros((CHUNKS, LANES), F32) for _ in range(2)]
        for g in range(GROUPS):
            for s in range(2):
                sums = piece_sums(piece[g] * piece[g], lane8, *segment(g, s))
                squares = [jnp.where(lane8 == 2 * g + s, sums[par], squares[par]) for par in range(2)]
        for par in range(2):
            packed[par, at, :] = squares[par]

    pair = (col // 2) * 2
    partner = pair + 1 - lax.rem(col, 2)
    chips = cols // 2

    def arrived(i):
        away = jnp.where(lax.rem(i, 2) == 1, (i + 1) // 2, chips - i // 2)
        src = lax.rem(pair + 2 * away, cols)
        copy3(src, src).wait_recv()
        copy3(src + 1, src + 1).wait_recv()
        return src

    def work(src):
        for b in (src, src + 1):
            square_sums(b)
        for b in (src, src + 1):
            partial(b)

    copy3(partner, partner).wait_recv()
    final = pair
    if chips > 1:
        work(pair)
        lax.fori_loop(1, chips - 1, lambda i, _: (work(arrived(i)), 0)[1], 0)
        final = arrived(jnp.int32(chips - 1))
    square_sums(final)
    square_sums(final + 1)
    vectors = [recv3[:, g].reshape(half, LANES) for g in range(GROUPS)]
    lane = lax.broadcasted_iota(jnp.int32, (half, LANES), 1)
    square_out[...] = jnp.concatenate([packed[0], packed[1]], axis=0).T[:2 * GROUPS, :]

    def square_copy(way, to):
        return pltpu.make_async_remote_copy(
            src_ref=square_out, dst_ref=square_in.at[way], send_sem=st.at[way], recv_sem=rt.at[way],
            device_id={"row": to}, device_id_type=MESH,
        )

    square_copies = [square_copy(0, left), square_copy(1, right)]
    for c in square_copies:
        c.start()
    partial(final)
    partial(final + 1)

    blocks = rows // LANES
    part = half // PIECES
    steps = [(n, q, par) for n in range(blocks) for q in range(PIECES) for par in range(2)]
    last = me == parts - 1
    first = me == 0

    def exchange(g, n, way, par, q):
        to = left if way == 0 else right
        at = pl.ds(q * part, part)
        return pltpu.make_async_remote_copy(
            src_ref=send4.at[g, n, way, par, at], dst_ref=recv4.at[g, n, way, par, at],
            send_sem=s4.at[g, n, way, par, q], recv_sem=r4.at[g, n, way, par, q],
            device_id={"row": to}, device_id_type=MESH,
        )

    def line(q, g, s, par):
        return pl.ds(q * part * SUMS + 4 * g + 2 * s + par, part, stride=SUMS)

    def prepare(g, n, q, par):
        tiles = pl.ds(q * part, part)
        for s in range(2):
            x = raw[n, line(q, g, s, par), :]
            for k, (pg, ps, h, t, _, _) in enumerate(PAIRS):
                if (pg, ps) == (g, s):
                    x = x - gram[k, par, tiles] * coef_ref[n, line(q, h, t, par), :]
            send4[g, n, s, par, tiles] = x
        exchange(g, n, 0, par, q).start()
        exchange(g, n, 1, par, q).start()

    def of_next(x, par):
        return jnp.where(last, pltpu.roll(x, half - 1, 0), x) if par else x

    def of_previous(x, par):
        return x if par else jnp.where(first, pltpu.roll(x, 1, 0), x)

    def next_parity(par):
        return jnp.where(last, 1 - par, par)

    def previous_parity(par):
        return jnp.where(first, 1 - par, par)

    def heads_after(g, n, q, par):
        from_ref = recv4.at[g, n, 0, next_parity(par)]
        if par == 0:
            exchange(g, n, 0, next_parity(par), q).wait_recv()
            return from_ref[q * part:(q + 1) * part]

        @pl.when(jnp.logical_not(last))
        def _():
            exchange(g, n, 0, 1, q).wait_recv()

        @pl.when(last)
        def _():
            if q == 0:
                exchange(g, n, 0, 0, 0).wait_recv()
            if q + 1 < PIECES:
                exchange(g, n, 0, 0, q + 1).wait_recv()

        def shifted():
            if q + 1 < PIECES:
                return from_ref[q * part + 1:(q + 1) * part + 1]
            return pltpu.roll(from_ref[q * part:(q + 1) * part], part - 1, 0)

        return lax.cond(last, shifted, lambda: from_ref[q * part:(q + 1) * part])

    def tails_before(g, n, q, par):
        from_ref = recv4.at[g, n, 1, previous_parity(par)]
        exchange(g, n, 1, previous_parity(par), q).wait_recv()
        if par:
            return from_ref[q * part:(q + 1) * part]

        def shifted():
            if q:
                return from_ref[q * part - 1:(q + 1) * part - 1]
            return pltpu.roll(from_ref[0:part], 1, 0)

        return lax.cond(first, shifted, lambda: from_ref[q * part:(q + 1) * part])

    def finish(g, n, q, par):
        tiles = pl.ds(q * part, part)
        after = heads_after(g, n, q, par)
        before = tails_before(g, n, q, par)
        head, tail = send4[g, n, 0, par, tiles], send4[g, n, 1, par, tiles]
        coef_ref[n, line(q, g, 0, par), :] = tau[2 * g, par, tiles] * (before + head)
        coef_ref[n, line(q, g, 1, par), :] = tau[2 * g + 1, par, tiles] * (tail + after)

    for n, q, par in steps:
        prepare(0, n, q, par)

    for k, (g, s, h, t, lo, hi) in enumerate(PAIRS):
        sums = piece_sums(vectors[g] * vectors[h], lane, lo, hi)
        for par in range(2):
            gram[k, par] = jnp.broadcast_to(sums[par], (half, LANES))

    for c in square_copies:
        c.wait()

    def turned(way):
        full = jnp.concatenate([square_in[way]] * (2 * half // (2 * GROUPS)), axis=0).T
        return [full[:half], full[half:]]

    right_squares, left_squares = turned(0), turned(1)
    at = lax.broadcasted_iota(jnp.int32, (half, 1), 0)
    for par in range(2):
        after = of_next(jnp.where(last, right_squares[1 - par], right_squares[par]), par)
        before = of_previous(jnp.where(first, left_squares[1 - par], left_squares[par]), par)
        here = packed[par]
        for g in range(GROUPS):
            head, tail = slice(2 * g, 2 * g + 1), slice(2 * g + 1, 2 * g + 2)
            own = 2.0 / (here[:, tail] + after[:, head] + 1e-06)
            prior = 2.0 / (before[:, tail] + here[:, head] + 1e-06)
            if par:
                own = jnp.where(last & (at == half - 1), 0.0, own)
            else:
                prior = jnp.where(first & (at == 0), 0.0, prior)
            tau[2 * g, par] = jnp.broadcast_to(prior, (half, LANES))
            tau[2 * g + 1, par] = jnp.broadcast_to(own, (half, LANES))

    for g in range(GROUPS):
        for n, q, par in steps:
            finish(g, n, q, par)
            if g + 1 < GROUPS:
                prepare(g + 1, n, q, par)

    wait_for(send_a, parts - 1, sa)
    each_other(1, lambda i: copy_b(i).wait_send())
    each_other(0, lambda i: pick_copy_a(i).wait_send())

    @pl.when(odd)
    def _():
        wait_for(pick_b, parts - 1, spb)

    others(cols, col, lambda to: copy3(to, col).wait_send())
    for g in range(GROUPS):
        for n, q, par in steps:
            exchange(g, n, 0, par, q).wait_send()
            exchange(g, n, 1, par, q).wait_send()


def coefficients(parts, cols, owner, stored, slab):
    rows, length = slab.shape
    half = length // LANES
    vmem, dma = pltpu.VMEM, pltpu.SemaphoreType.DMA
    blocks = rows // LANES
    piece = (cols, GROUPS, CHUNKS, LANES)
    return pl.pallas_call(
        functools.partial(coef_kernel, parts, cols),
        name="coefficients",
        out_shape=(
            jax.ShapeDtypeStruct((blocks, half * SUMS, LANES), F32),
            jax.ShapeDtypeStruct((cols, CHUNKS // 2, 4 * SUMS, PAIR), BF16),
            jax.ShapeDtypeStruct((cols, rows, WIDE), F32),
        ),
        in_specs=[
            pl.BlockSpec(memory_space=pltpu.HBM),
            pl.BlockSpec(memory_space=pltpu.HBM),
            pl.BlockSpec(memory_space=pltpu.HBM),
        ],
        out_specs=(pl.BlockSpec(memory_space=vmem),) * 3,
        scratch_shapes=[
            pltpu.SMEM((GROUPS,), jnp.int32),
            vmem(stored.shape, F32),
            vmem((cols, rows, WIDE), BF16),
            vmem((cols, rows, WIDE), BF16),
            vmem((parts, cols // 2, CHUNKS, LANES), F32),
            vmem((parts, cols // 2, CHUNKS, LANES), F32),
            vmem((cols // 2, parts, CHUNKS, LANES), F32),
            vmem((cols, parts, CHUNKS, LANES), F32),
            vmem((cols // 2, GROUPS, CHUNKS, LANES), F32),
            vmem((cols, GROUPS, CHUNKS, LANES), F32),
            vmem((parts, GROUPS, CHUNKS, LANES), F32),
            vmem((parts, GROUPS, CHUNKS, LANES), F32),
            vmem(piece, F32),
            vmem((blocks, half * SUMS, LANES), F32),
            vmem((2, half, LANES), F32),
            vmem((2 * GROUPS, 2 * half), F32),
            vmem((2, 2 * GROUPS, 2 * half), F32),
            vmem((len(PAIRS), 2, half, LANES), F32),
            vmem((2 * GROUPS, 2, half, LANES), F32),
            vmem((GROUPS, blocks, 2, 2, half, LANES), F32),
            vmem((GROUPS, blocks, 2, 2, half, LANES), F32),
            dma, dma, dma((cols,)),
            dma, dma, dma((cols // 2,)), dma,
            dma((cols // 2,)), dma, dma, dma,
            dma((cols,)), dma((cols,)),
            dma((2,)), dma((2,)),
            dma((GROUPS, blocks, 2, 2, PIECES)), dma((GROUPS, blocks, 2, 2, PIECES)),
        ],
        compiler_params=pltpu.CompilerParams(
            has_side_effects=True, collective_id=0, vmem_limit_bytes=40 * 1024 * 1024
        ),
    )(*(pltpu.with_memory_space_constraint(x, pltpu.HBM) for x in (owner, stored, slab)))


def update_kernel(cols, coef_ref, spread_ref, slab_ref, out_ref, ready, sem):
    slots = ready.shape[0]

    rows = ready.shape[1] // OUT_CUTS

    def cut(b, k):
        slot = lax.rem(b, slots)
        at = pl.ds(pl.multiple_of(b * WIDE, WIDE), WIDE)
        some = pl.ds(k * rows, rows)
        return pltpu.make_async_copy(ready.at[slot, some], out_ref.at[some, at], sem.at[slot, k])

    def start(b):
        for k in range(OUT_CUTS):
            cut(b, k).start()

    def wait(b):
        for k in range(OUT_CUTS):
            cut(b, k).wait()

    def block(b):
        lines = CHUNKS * SUMS
        at = pl.ds(pl.multiple_of(b * lines, lines), lines)
        high, low = split(jnp.concatenate([coef_ref[n, at, :] for n in range(coef_ref.shape[0])], axis=1))
        stack = []
        for t in range(CHUNKS // 2):
            at = slice(t * 2 * SUMS, (t + 1) * 2 * SUMS)
            stack += [high[at], high[at], low[at], low[at]]
        turned = jnp.concatenate(stack, axis=0).T
        for t in range(CHUNKS // 2):
            both = spread_ref[b, t]
            depth = 2 * both.shape[0]
            change = jnp.dot(
                turned[:, t * depth:(t + 1) * depth], jnp.concatenate([both, both], axis=0),
                preferred_element_type=F32,
            )
            at = slice(t * PAIR, (t + 1) * PAIR)
            ready[lax.rem(b, slots), :, at] = slab_ref[b, :, at] - change

    def two(i, _):
        @pl.when(i >= slots // 2)
        def _():
            wait(2 * i - slots)
            wait(2 * i + 1 - slots)

        block(2 * i)
        start(2 * i)
        block(2 * i + 1)
        start(2 * i + 1)
        return 0

    lax.fori_loop(0, cols // 2, two, 0)
    lax.fori_loop(max(cols - slots, 0), cols, lambda b, _: (wait(b), 0)[1], 0)


def update(cols, coef, wide, slab_in):
    blocks, rows, length = slab_in.shape
    return pl.pallas_call(
        functools.partial(update_kernel, cols),
        name="update",
        out_shape=jax.ShapeDtypeStruct((rows, blocks * length), F32),
        in_specs=[pl.BlockSpec(memory_space=pltpu.VMEM)] * 3,
        out_specs=pl.BlockSpec(memory_space=pltpu.HBM),
        scratch_shapes=[pltpu.VMEM((4, rows, length), F32), pltpu.SemaphoreType.DMA((4, OUT_CUTS))],
        compiler_params=pltpu.CompilerParams(vmem_limit_bytes=24 * 1024 * 1024),
    )(coef, wide, slab_in)


def shards(parts, cols, slab, stored, owner):
    coef, wide, slab_in = coefficients(parts, cols, owner, stored.reshape(-1, LANES), slab)
    return update(cols, coef, wide, slab_in)


def solution(mesh):
    placed = (P("col", "row"), P(("row", "col"), None), P())
    body = functools.partial(shards, mesh.shape["row"], mesh.shape["col"])
    return jax.shard_map(
        body, mesh=mesh, in_specs=placed, out_specs=P("col", "row"), check_vma=False
    )
```
